256 devices in a mesh: img: 32 (over y, z), ori: 8 (over x, core).
Axes of the slice: x: 4, y: 4, z: 8, core: 2. Of those that a mesh axis runs over, the one named last changes fastest.
Arguments:
- images: bfloat16 [1024, 2, 16256], P('img'), may hold values from -6 to 6
- shifts: int32 [1024], P('img'), may hold values from 0 to 35
- inv_temp: float32 [1024], P('img'), may hold values from 0.5 to 4
- candidates: int32 [32, 512], P('img'), may hold values from 0 to 1023
- volume: bfloat16 [64, 2, 16256], P(None, None, 'img'), may hold values from -6 to 6
- tilts: bfloat16 [1024, 64], P('ori'), may hold values from -1 to 1
- azimuth: float32 [1024], P('ori'), may hold values from -3.140625 to 3.140625
Outputs:
- posteriors: float32 [1024, 1024], P('img', 'ori')
- weighted_sums: float32 [16256, 2, 1024], P('img', None, 'ori')
- volume_grad: float32 [64, 2, 16256], P(None, None, 'img')
The draws below stay inside these ranges and needn't reach their ends.
Inputs may be any that keep to these rules, and one draw needn't show every extreme that they name: `candidates`: A group's list may name an orientation more than once.
All inputs are finite; a program needn't handle non-finite values.
Results may differ from the reference program's by a relative error of at most 0.017.
Values may be sent and summed in bfloat16 or wider, within the bound.
No kernel may reach another device: no remote copies, remote signals or barrier semaphores. Data moves between devices by JAX's collectives and lax.ppermute only.
A program may use at most 128 MiB of HBM per device.

```python
import math
import jax
import jax.numpy as jnp
import numpy as np
from jax import lax

KH = 16256
NDEG = 64
ORIENT = 1024
NSHIFT = 36
NCAND = 512
IMG_DEV = 32
GROUPS = 32
IMAGES = 1024


def draw_images(key, part):
    own_key = jax.random.fold_in(key, 101)
    entries = jnp.clip(jax.random.normal(own_key, (IMAGES, 2, KH), jnp.float32), -6.0, 6.0)
    return entries.astype(jnp.bfloat16)


def draw_volume(key, part):
    own_key = jax.random.fold_in(key, 211)
    entries = jnp.clip(jax.random.normal(own_key, (NDEG, 2, KH), jnp.float32), -6.0, 6.0)
    return entries.astype(jnp.bfloat16)


def draw_tilts(key, part):
    own_key = jax.random.fold_in(key, 307)
    entries = jax.random.normal(own_key, (ORIENT, NDEG), jnp.float32)
    length = jnp.sqrt(jnp.sum(entries * entries, axis=1, keepdims=True))
    return (entries / length).astype(jnp.bfloat16)


def draw_inv_temp(key, part):
    own_key = jax.random.fold_in(key, 409)
    base_key, hot_key, pick_key = jax.random.split(own_key, 3)
    base = jnp.exp(jax.random.uniform(base_key, (IMAGES,), jnp.float32, jnp.log(0.5), jnp.log(2.0)))
    low_hot = 150.0 * 128.0 / KH
    high_hot = 400.0 * 128.0 / KH
    hot = jnp.exp(jax.random.uniform(hot_key, (IMAGES,), jnp.float32, jnp.log(low_hot), jnp.log(high_hot)))
    position = jnp.arange(IMAGES, dtype=jnp.int32)
    chosen = jnp.logical_or(position % IMG_DEV == 0, jax.random.uniform(pick_key, (IMAGES,), jnp.float32) < 0.1)
    values = jnp.where(chosen, hot, base)
    return jnp.clip(values, 0.5, max(2.0, float(51200 // KH + 1))).astype(jnp.float32)


def with_ends(array, key, low, top_value):
    shape = array.shape
    spot = [jax.random.randint(jax.random.fold_in(key, axis), (), 0, shape[axis]) for axis in range(len(shape))]
    array = array.at[tuple(spot)].set(low)
    longest = shape.index(max(shape))
    spot[longest] = (spot[longest] + 1) % shape[longest]
    return array.at[tuple(spot)].set(top_value)


def rank_table(amount, lean):
    loads = [(1 << 20) // math.isqrt(standing ** lean) + 1 for standing in range(1, amount + 1)]
    scale = 1 + sum(loads) // (1 << 30)
    return np.cumsum(np.array([max(1, weight // scale) for weight in loads]))


def skewed_ids(key, shape, amount, skew):
    listing = rank_table(amount, skew)
    ticket = jax.random.randint(jax.random.fold_in(key, 1), shape, 0, int(listing[amount - 1]))
    standing = jnp.searchsorted(jnp.asarray(listing, jnp.int32), ticket, side="right")
    return jax.random.permutation(jax.random.fold_in(key, 2), amount)[standing].astype(jnp.int32)


def setup_inputs(seed: int = 0) -> dict:
    splits = jax.random.split(jax.random.key(seed), 8)
    images = draw_images(jax.random.fold_in(splits[7], 71), 0)
    shifts = with_ends(jax.random.randint(splits[1], (IMAGES,), 0, NSHIFT), jax.random.fold_in(splits[1], 1), 0, NSHIFT - 1).astype(jnp.int32)
    inv_temp = draw_inv_temp(jax.random.fold_in(splits[7], 71), 0)
    candidates = with_ends(skewed_ids(splits[3], (GROUPS, NCAND), ORIENT, 1), jax.random.fold_in(splits[3], 3), 0, ORIENT - 1).astype(jnp.int32)
    volume = draw_volume(jax.random.fold_in(splits[7], 71), 0)
    tilts = draw_tilts(jax.random.fold_in(splits[7], 71), 0)
    azimuth = jnp.clip(jax.random.uniform(splits[6], (ORIENT,), jnp.float32, -3.140625, 3.140625), -3.140625, 3.140625)
    return dict(images=images, shifts=shifts, inv_temp=inv_temp, candidates=candidates, volume=volume, tilts=tilts, azimuth=azimuth)


noise_var = 128.0
masked_fill = -1.0e30


def order_table(start, width):
    return ((start + jnp.arange(width, dtype=jnp.int32)) % 64 - 32).astype(jnp.float32)


def project_piece(piece, start, tilts, azimuth):
    width = piece.shape[2]
    degrees = piece.shape[0]
    mixed = jnp.dot(tilts, piece.reshape(degrees, 2 * width), preferred_element_type=jnp.float32)
    mixed = mixed.reshape(tilts.shape[0], 2, width)
    angles = azimuth[:, None] * order_table(start, width)[None, :]
    cosine = jnp.cos(angles)
    sine = jnp.sin(angles)
    real_part = mixed[:, 0] * cosine - mixed[:, 1] * sine
    imag_part = mixed[:, 0] * sine + mixed[:, 1] * cosine
    return jnp.stack([real_part, imag_part], axis=1).astype(jnp.bfloat16)


def rotate_images(images, shifts):
    width = images.shape[2]
    phase = shifts.astype(jnp.float32) * (2.0 * math.pi / NSHIFT)
    angles = phase[:, None] * order_table(0, width)[None, :]
    cosine = jnp.cos(angles)
    sine = jnp.sin(angles)
    first = images[:, 0].astype(jnp.float32)
    second = images[:, 1].astype(jnp.float32)
    real_part = first * cosine - second * sine
    imag_part = first * sine + second * cosine
    return jnp.stack([real_part, imag_part], axis=1).astype(jnp.bfloat16)


def reference(images, shifts, inv_temp, candidates, volume, tilts, azimuth):
    slices = project_piece(volume, 0, tilts, azimuth)
    flat_slices = slices.reshape(ORIENT, 2 * KH)
    energies = jnp.sum(jnp.square(slices.astype(jnp.float32)), axis=(1, 2))
    orient_ids = jnp.arange(ORIENT, dtype=jnp.int32)
    grouped = images.reshape(GROUPS, IMG_DEV, 2, KH)
    group_shifts = shifts.reshape(GROUPS, IMG_DEV)
    group_temps = inv_temp.reshape(GROUPS, IMG_DEV)

    def visit(carry, item):
        sums, mass = carry
        block, shift_row, temp_row, cand_row = item
        rotated = rotate_images(block, shift_row)
        inner = jnp.dot(rotated.reshape(IMG_DEV, 2 * KH), flat_slices.T, preferred_element_type=jnp.float32)
        scores = temp_row[:, None] * (inner - 0.5 * energies[None, :]) / noise_var
        allowed = jnp.any(cand_row[:, None] == orient_ids[None, :], axis=0)
        allowed_rows = jnp.broadcast_to(allowed[None, :], scores.shape)
        held = jnp.where(allowed_rows, scores, masked_fill)
        peak = jnp.max(held, axis=1)
        expo = jnp.where(allowed_rows, jnp.exp(held - peak[:, None]), 0.0)
        total = jnp.sum(expo, axis=1)
        posts = expo / total[:, None]
        post_bf = posts.astype(jnp.bfloat16)
        term = jnp.einsum("ick,io->kco", rotated.astype(jnp.float32), post_bf.astype(jnp.float32))
        term_bf = lax.optimization_barrier(term.astype(jnp.bfloat16))
        return (sums + term_bf.astype(jnp.float32), mass + jnp.sum(posts, axis=0)), posts

    start_sums = jnp.zeros((KH, 2, ORIENT), jnp.float32)
    start_mass = jnp.zeros((ORIENT,), jnp.float32)
    (sums, mass), posts = lax.scan(visit, (start_sums, start_mass), (grouped, group_shifts, group_temps, candidates))
    posteriors = posts.reshape(GROUPS * IMG_DEV, ORIENT)
    own = jnp.transpose(slices.astype(jnp.float32), (2, 1, 0))
    resid = sums - mass[None, None, :] * own
    angles = order_table(0, KH)[:, None] * azimuth[None, :]
    cosine = jnp.cos(angles)
    sine = jnp.sin(angles)
    back_real = resid[:, 0] * cosine + resid[:, 1] * sine
    back_imag = resid[:, 1] * cosine - resid[:, 0] * sine
    back = jnp.stack([back_real, back_imag], axis=1)
    volume_grad = jnp.einsum("kco,ol->lck", back, tilts.astype(jnp.float32), precision=lax.Precision.HIGHEST) / noise_var
    return posteriors, sums, volume_grad
```

```python
import math

import jax
import jax.numpy as jnp
from jax import lax
from jax.experimental import pallas as pl
from jax.experimental.pallas import tpu as pltpu
from jax.sharding import Mesh
from jax.sharding import PartitionSpec as P

NSHIFT = 36
LANES = 128
ROWS = 8
ORDERS = 64
noise_var = 128.0
masked_fill = -1e30
ORI = ("x", "c")


def call(kernel, out_shape, scalars, *args, flops=0):
    specs = [pl.BlockSpec(memory_space=pltpu.SMEM)] + [pl.BlockSpec(memory_space=pltpu.VMEM)] * len(args)
    outs = jax.tree.map(lambda _: pl.BlockSpec(memory_space=pltpu.VMEM), out_shape)
    moved = sum(a.size * a.dtype.itemsize for a in (*args, *jax.tree.leaves(out_shape)))
    return pl.pallas_call(
        kernel,
        out_shape=out_shape,
        in_specs=specs,
        out_specs=outs,
        cost_estimate=pl.CostEstimate(flops=flops, transcendentals=0, bytes_accessed=moved),
    )(scalars, *args)


def shape(dims, dtype=jnp.float32):
    return jax.ShapeDtypeStruct(dims, dtype)


def across(x, axis, step):
    count = lax.axis_size(axis)
    return lax.ppermute(x, axis, [(s, (s + step) % count) for s in range(count)])


def rotate_and_cut(width, parts):
    tiles = -(-width // LANES)

    def kernel(_, re_ref, im_ref, a_ref, b_ref, out_ref):
        a, b = a_ref[...], b_ref[...]
        lane = lax.broadcasted_iota(jnp.int32, (ROWS, LANES), 1)
        whole = re_ref.shape[1] // LANES
        turned = []
        for k in range(whole):
            at = slice(k * LANES, (k + 1) * LANES)
            turned.append(re_ref[:, at].astype(jnp.float32) * a + im_ref[:, at].astype(jnp.float32) * b)
        for part in range(parts):
            shift = (part * width) % LANES
            for t in range(tiles):
                first = part * width // LANES + t
                one = turned[first]
                if shift:
                    two = turned[min(first + 1, whole - 1)]
                    one = jnp.where(lane < shift, two, one)
                    one = pltpu.roll(one, LANES - shift, 1)
                left = width - t * LANES
                if left < LANES:
                    one = jnp.where(lane < left, one, 0.0)
                out_ref[part, t] = one.astype(jnp.bfloat16)

    return kernel


def wide(ref, rows):
    tiles = ref.shape[1] // ROWS
    pieces = [ref[:, t * ROWS : (t + 1) * ROWS, :].reshape(rows, LANES) for t in range(tiles)]
    return jnp.concatenate(pieces, axis=1)


def inner_kernel(s_ref, own_ref, other_ref, slices_ref, half_ref, out_ref):
    c = s_ref[0]
    groups = own_ref.shape[0]
    rows = groups * ROWS
    own, other = wide(own_ref, rows), wide(other_ref, rows)
    dims = (((1,), (1,)), ((), ()))
    for d in range(slices_ref.shape[1]):
        acc = lax.dot_general(own, slices_ref[c, d], dims, preferred_element_type=jnp.float32)
        acc += lax.dot_general(other, slices_ref[1 - c, d], dims, preferred_element_type=jnp.float32)
        acc = acc - half_ref[d : d + 1, :]
        out_ref[:, d * ROWS : (d + 1) * ROWS, :] = acc.reshape(groups, ROWS, LANES)


def stats_kernel(_, parts_ref, temp_ref, allowed_ref, held_ref, stats_ref):
    inner = parts_ref[0]
    for g in range(1, parts_ref.shape[0]):
        inner = inner + parts_ref[g]
    allowed = allowed_ref[...] > 0.5
    held = jnp.where(allowed, temp_ref[...] * inner / noise_var, masked_fill)
    held_ref[...] = held
    blocks = held.shape[0] // ROWS
    top = jnp.max(held.reshape(blocks, ROWS, LANES), axis=0)
    peak = jnp.broadcast_to(jnp.max(top, axis=1, keepdims=True), (ROWS, LANES))
    full = jnp.concatenate([peak] * blocks, axis=0)
    expo = jnp.where(allowed, jnp.exp(held - full), 0.0)
    total = jnp.sum(jnp.sum(expo.reshape(blocks, ROWS, LANES), axis=0), axis=1, keepdims=True)
    stats_ref[0] = peak
    stats_ref[1] = jnp.broadcast_to(total, (ROWS, LANES))


def posts_kernel(_, held_ref, allowed_ref, mine_ref, theirs_ref, *out_refs):
    peak = jnp.maximum(mine_ref[0], theirs_ref[0])
    total = mine_ref[1] * jnp.exp(mine_ref[0] - peak) + theirs_ref[1] * jnp.exp(theirs_ref[0] - peak)
    for d, out_ref in enumerate(out_refs):
        at = slice(d * ROWS, (d + 1) * ROWS)
        out_ref[...] = jnp.where(allowed_ref[at, :] > 0.5, jnp.exp(held_ref[at, :] - peak) / total, 0.0)


def spread_kernel(s_ref, *refs):
    count = len(refs) - 2
    blocks, (post_ref, copies_ref) = refs[:count], refs[count:]
    x = s_ref[1]
    rounded = jnp.concatenate([b[...] for b in blocks], axis=0).astype(jnp.bfloat16)
    for e, block in enumerate(blocks):
        at = lax.rem(x + count - e, count) * ROWS
        post_ref[pl.ds(pl.multiple_of(at, ROWS), ROWS), :] = block[...]
    for g in range(copies_ref.shape[0]):
        copies_ref[g] = rounded


def final_kernel(s_ref, post_ref, slices_ref, cos_ref, sin_ref, turned_ref, *refs):
    c = s_ref[0]
    images, (sums_ref, mine_ref, theirs_ref) = refs[:-3], refs[-3:]
    own, other = images[: len(images) // 2], images[len(images) // 2 :]
    groups = post_ref.shape[0]
    rows = groups * ROWS
    posts = [
        post_ref[:, e * ROWS : (e + 1) * ROWS, :].reshape(rows, LANES).astype(jnp.float32).T for e in range(len(own))
    ]
    posts = jnp.concatenate(posts, axis=1)
    mass = jnp.sum(posts, axis=1, keepdims=True)
    posts = posts.astype(jnp.bfloat16)
    tiles = own[0].shape[1] // ROWS
    for where, blocks in ((c, own), (1 - c, other)):
        for t in range(tiles):
            piece = jnp.concatenate(
                [b[:, t * ROWS : (t + 1) * ROWS, :].reshape(rows, LANES) for b in blocks], axis=0
            )
            sums_ref[where, :, t * LANES : (t + 1) * LANES] = jnp.dot(
                posts, piece, preferred_element_type=jnp.float32
            )
    cosine, sine = cos_ref[...], sin_ref[...]
    for t in range(tiles):
        at = slice(t * LANES, (t + 1) * LANES)
        first = sums_ref[0, :, at] - mass * slices_ref[0, 0, :, at].astype(jnp.float32)
        second = sums_ref[1, :, at] - mass * slices_ref[1, 0, :, at].astype(jnp.float32)
        grads = []
        for back in (first * cosine + second * sine, second * cosine - first * sine):
            high = back.astype(jnp.bfloat16)
            low = (back - high.astype(jnp.float32)).astype(jnp.bfloat16)
            both = jnp.concatenate([high, low], axis=0)
            grads.append(jnp.dot(turned_ref[...], both, preferred_element_type=jnp.float32) / noise_var)
        mine_ref[:, at] = jnp.where(c == 0, grads[0], grads[1])
        theirs_ref[:, at] = jnp.where(c == 0, grads[1], grads[0]).astype(jnp.bfloat16)


def weave_kernel(_, sums_ref, out_ref):
    width = out_ref.shape[0] // 2
    for part in range(2):
        for t in range(sums_ref.shape[2] // LANES):
            count = min(LANES, width - t * LANES)
            block = sums_ref[part, :, t * LANES : (t + 1) * LANES].T
            out_ref[pl.ds(2 * t * LANES + part, count, stride=2), :] = block[:count]


def shards(images, shifts, inv_temp, candidates, volume, tilts, azimuth):
    i, x, c = (lax.axis_index(a) for a in ("img", "x", "c"))
    groups, across_x = lax.axis_size("img"), lax.axis_size("x")
    orients, degrees = tilts.shape
    width = volume.shape[2]
    padded = -(-width // LANES) * LANES
    tiles = padded // LANES
    scalars = jnp.stack([c, x]).astype(jnp.int32)

    own = lax.dynamic_slice_in_dim(images, x * ROWS, ROWS, 0)
    own_shifts = lax.dynamic_slice_in_dim(shifts, x * ROWS, ROWS, 0)
    own_temp = lax.dynamic_slice_in_dim(inv_temp, x * ROWS, ROWS, 0)
    order = (jnp.arange(LANES, dtype=jnp.int32) % ORDERS - ORDERS // 2).astype(jnp.float32)
    angles = own_shifts.astype(jnp.float32)[:, None] * (2.0 * math.pi / NSHIFT) * order[None, :]
    cosine, sine = jnp.cos(angles), jnp.sin(angles)
    by_real = jnp.where(c == 0, cosine, sine)
    by_imag = jnp.where(c == 0, -sine, cosine)
    cut = call(
        rotate_and_cut(width, groups),
        shape((groups, tiles, ROWS, LANES), jnp.bfloat16),
        scalars,
        own[:, 0],
        own[:, 1],
        by_real,
        by_imag,
    )
    mine = lax.all_to_all(cut.reshape(groups, tiles * ROWS, LANES), "img", 0, 0, tiled=True)
    other = across(mine, "c", 1)

    packed = jnp.concatenate(
        [tilts.astype(jnp.float32), azimuth[:, None], jnp.zeros((orients, LANES - degrees - 1), jnp.float32)], axis=1
    )
    gathered = jnp.stack([packed] + [across(packed, "x", -d) for d in range(1, across_x)])
    all_tilts = gathered[:, :, :degrees].astype(jnp.bfloat16)
    order = ((i * width + jnp.arange(LANES, dtype=jnp.int32)) % ORDERS - ORDERS // 2).astype(jnp.float32)
    angles = gathered[:, :, degrees : degrees + 1] * order[None, None, :]
    cosine, sine = jnp.cos(angles), jnp.sin(angles)
    pad = jnp.pad(volume, ((0, 0), (0, 0), (0, padded - width)))
    mixed = jnp.einsum("dol,lcq->cdoq", all_tilts, pad, preferred_element_type=jnp.float32)
    mixed = mixed.reshape(2, across_x, orients, tiles, LANES)
    turn_re, turn_im = cosine[:, :, None, :], sine[:, :, None, :]
    slices = jnp.stack([mixed[0] * turn_re - mixed[1] * turn_im, mixed[0] * turn_im + mixed[1] * turn_re])
    slices = slices.reshape(2, across_x, orients, padded).astype(jnp.bfloat16)
    half = 0.5 * jnp.sum(jnp.square(slices.astype(jnp.float32)), axis=(0, 3))

    partial = call(
        inner_kernel,
        shape((groups, across_x * ROWS, LANES)),
        scalars,
        mine,
        other,
        slices,
        half,
        flops=4 * groups * ROWS * padded * across_x * LANES,
    )
    partial = lax.all_to_all(partial, "img", 0, 0, tiled=True)

    ids = ((x + jnp.arange(across_x)) % across_x * 2 + c)[:, None] * orients + jnp.arange(orients)[None, :]
    allowed = jnp.any(candidates[0][:, None] == ids.reshape(1, -1), axis=0).astype(jnp.float32)
    allowed = jnp.broadcast_to(allowed.reshape(across_x, 1, orients), (across_x, ROWS, orients)).reshape(-1, orients)
    temp = jnp.broadcast_to(jnp.tile(own_temp, across_x)[:, None], (across_x * ROWS, LANES))
    held, stats = call(
        stats_kernel, (shape((across_x * ROWS, LANES)), shape((2, ROWS, LANES))), scalars, partial, temp, allowed
    )
    blocks = call(
        posts_kernel, [shape((ROWS, LANES))] * across_x, scalars, held, allowed, stats, across(stats, "c", 1)
    )
    blocks = [blocks[0]] + [across(blocks[d], "x", d) for d in range(1, across_x)]
    posteriors, copies = call(
        spread_kernel,
        (shape((across_x * ROWS, LANES)), shape((groups, across_x * ROWS, LANES), jnp.bfloat16)),
        scalars,
        *blocks,
    )
    posts = lax.all_to_all(copies, "img", 0, 0, tiled=True)

    mine_all = [mine] + [across(mine, "x", d) for d in range(1, across_x)]
    other_all = [other] + [across(m, "c", 1) for m in mine_all[1:]]
    turned = jnp.concatenate([tilts.T, tilts.T], axis=1)
    sums, grad, theirs = call(
        final_kernel,
        (shape((2, orients, padded)), shape((degrees, padded)), shape((degrees, padded), jnp.bfloat16)),
        scalars,
        posts,
        slices[:, :1],
        cosine[0],
        sine[0],
        turned,
        *mine_all,
        *other_all,
        flops=4 * groups * across_x * ROWS * padded * orients,
    )
    woven = call(weave_kernel, shape((2 * width, orients)), scalars, sums)
    weighted_sums = woven.reshape(width, 2, orients)

    grad = (grad + across(theirs, "c", 1).astype(jnp.float32)).astype(jnp.bfloat16)
    grads = [grad] + [across(grad, "x", d) for d in range(1, across_x)]
    grad = sum(g.astype(jnp.float32) for g in grads)
    theirs = across(grad, "c", 1)
    volume_grad = jnp.stack([jnp.where(c == 0, grad, theirs), jnp.where(c == 0, theirs, grad)], axis=1)
    return posteriors, weighted_sums, volume_grad[:, :, :width]


def solution(mesh):
    ori = mesh.shape["ori"]
    finer = Mesh(mesh.devices.reshape(mesh.shape["img"], ori // 2, 2), ("img", "x", "c"))
    return jax.shard_map(
        shards,
        mesh=finer,
        in_specs=(
            P("img", None, None),
            P("img"),
            P("img"),
            P("img", None),
            P(None, None, "img"),
            P(ORI, None),
            P(ORI),
        ),
        out_specs=(P("img", ORI), P("img", None, ORI), P(None, None, "img")),
        check_vma=False,
    )
```

```python
import math

import jax
import jax.numpy as jnp
from jax import lax
from jax.experimental import pallas as pl
from jax.experimental.pallas import tpu as pltpu
from jax.sharding import Mesh
from jax.sharding import PartitionSpec as P


NSHIFT = 36
LANES = 128
ROWS = 8
ORDERS = 64
noise_var = 128.0
masked_fill = -1e30
ORI = ("x", "c")


def call(kernel, out_shape, scalars, *args, flops=0):
    specs = [pl.BlockSpec(memory_space=pltpu.SMEM)] + [pl.BlockSpec(memory_space=pltpu.VMEM)] * len(args)
    outs = jax.tree.map(lambda _: pl.BlockSpec(memory_space=pltpu.VMEM), out_shape)
    moved = sum(a.size * a.dtype.itemsize for a in (*args, *jax.tree.leaves(out_shape)))
    return pl.pallas_call(
        kernel,
        out_shape=out_shape,
        in_specs=specs,
        out_specs=outs,
        compiler_params=pltpu.CompilerParams(vmem_limit_bytes=8 * 2**20),
        cost_estimate=pl.CostEstimate(flops=flops, transcendentals=0, bytes_accessed=moved),
    )(scalars, *args)


def shape(dims, dtype=jnp.float32):
    return jax.ShapeDtypeStruct(dims, dtype)


def across(x, axis, step):
    count = lax.axis_size(axis)
    return lax.ppermute(x, axis, [(s, (s + step) % count) for s in range(count)])


def orders(start):
    lane = lax.broadcasted_iota(jnp.int32, (1, LANES), 1)
    return ((start + lane) % ORDERS - ORDERS // 2).astype(jnp.float32)


def rotate_and_cut(width, parts):
    tiles = -(-width // LANES)

    def kernel(s_ref, shifts_ref, images_ref, out_ref):
        c, x = s_ref[0], s_ref[1]
        row = lax.broadcasted_iota(jnp.int32, (ROWS, LANES), 0)
        phase = jnp.zeros((ROWS, LANES), jnp.float32)
        for n in range(ROWS):
            phase = jnp.where(row == n, shifts_ref[x * ROWS + n].astype(jnp.float32), phase)
        angles = phase * (2.0 * math.pi / NSHIFT) * orders(0)
        cosine, sine = jnp.cos(angles), jnp.sin(angles)
        a = jnp.where(c == 0, cosine, sine)
        b = jnp.where(c == 0, -sine, cosine)
        lane = lax.broadcasted_iota(jnp.int32, (ROWS, LANES), 1)
        whole = images_ref.shape[2] // LANES
        turned = []
        for k in range(whole):
            at = slice(k * LANES, (k + 1) * LANES)
            both = images_ref[:, :, at].astype(jnp.float32)
            turned.append(both[:, 0, :] * a + both[:, 1, :] * b)
        for part in range(parts):
            shift = (part * width) % LANES
            for t in range(tiles):
                first = part * width // LANES + t
                one = turned[first]
                if shift:
                    two = turned[min(first + 1, whole - 1)]
                    one = jnp.where(lane < shift, two, one)
                    one = pltpu.roll(one, LANES - shift, 1)
                left = width - t * LANES
                if left < LANES:
                    one = jnp.where(lane < left, one, 0.0)
                out_ref[part, t] = one.astype(jnp.bfloat16)

    return kernel


def cut_images(images, shifts, scalars, width, parts):
    tiles = -(-width // LANES)
    return pl.pallas_call(
        rotate_and_cut(width, parts),
        out_shape=shape((parts, tiles, ROWS, LANES), jnp.bfloat16),
        grid_spec=pltpu.PrefetchScalarGridSpec(
            num_scalar_prefetch=2,
            grid=(1,),
            in_specs=[pl.BlockSpec((ROWS, 2, images.shape[2]), lambda g, s, n: (s[1], 0, 0))],
            out_specs=pl.BlockSpec((parts, tiles, ROWS, LANES), lambda g, s, n: (0, 0, 0, 0)),
        ),
        compiler_params=pltpu.CompilerParams(vmem_limit_bytes=60 * 2**20),
    )(scalars, shifts, images)


def slices_kernel(width):
    def kernel(s_ref, packed_ref, volume_ref, slices_ref, half_ref, cos_ref, sin_ref):
        degrees = volume_ref.shape[1]
        order = orders(s_ref[2] * width)
        for d in range(packed_ref.shape[0]):
            block = packed_ref[d].T
            angles = jnp.broadcast_to(block[:, degrees : degrees + 1], block.shape) * order
            cosine, sine = jnp.cos(angles), jnp.sin(angles)
            if d == 0:
                cos_ref[...] = cosine
                sin_ref[...] = sine
            tilts = block[:, :degrees].astype(jnp.bfloat16)
            power = jnp.zeros_like(block)
            for t in range(volume_ref.shape[2] // LANES):
                at = slice(t * LANES, (t + 1) * LANES)
                re = jnp.dot(tilts, volume_ref[0, :, at], preferred_element_type=jnp.float32)
                im = jnp.dot(tilts, volume_ref[1, :, at], preferred_element_type=jnp.float32)
                first = (re * cosine - im * sine).astype(jnp.bfloat16)
                second = (re * sine + im * cosine).astype(jnp.bfloat16)
                slices_ref[0, d, :, at] = first
                slices_ref[1, d, :, at] = second
                power += jnp.square(first.astype(jnp.float32)) + jnp.square(second.astype(jnp.float32))
            half_ref[d : d + 1, :] = 0.5 * jnp.sum(power.T, axis=0, keepdims=True)

    return kernel


def wide(ref, rows):
    tiles = ref.shape[1] // ROWS
    pieces = [ref[:, t * ROWS : (t + 1) * ROWS, :].reshape(rows, LANES) for t in range(tiles)]
    return jnp.concatenate(pieces, axis=1)


def inner_kernel(s_ref, own_ref, other_ref, slices_ref, half_ref, out_ref):
    c = s_ref[0]
    groups = own_ref.shape[0]
    rows = groups * ROWS
    own, other = wide(own_ref, rows), wide(other_ref, rows)
    dims = (((1,), (1,)), ((), ()))
    for d in range(slices_ref.shape[1]):
        acc = lax.dot_general(own, slices_ref[c, d], dims, preferred_element_type=jnp.float32)
        acc += lax.dot_general(other, slices_ref[1 - c, d], dims, preferred_element_type=jnp.float32)
        acc = acc - half_ref[d : d + 1, :]
        out_ref[:, d * ROWS : (d + 1) * ROWS, :] = acc.reshape(groups, ROWS, LANES)


def stats_kernel(_, parts_ref, temp_ref, allowed_ref, held_ref, stats_ref):
    inner = parts_ref[0]
    for g in range(1, parts_ref.shape[0]):
        inner = inner + parts_ref[g]
    allowed = allowed_ref[...] > 0.5
    held = jnp.where(allowed, temp_ref[...] * inner / noise_var, masked_fill)
    held_ref[...] = held
    blocks = held.shape[0] // ROWS
    top = jnp.max(held.reshape(blocks, ROWS, LANES), axis=0)
    peak = jnp.broadcast_to(jnp.max(top, axis=1, keepdims=True), (ROWS, LANES))
    full = jnp.concatenate([peak] * blocks, axis=0)
    expo = jnp.where(allowed, jnp.exp(held - full), 0.0)
    total = jnp.sum(jnp.sum(expo.reshape(blocks, ROWS, LANES), axis=0), axis=1, keepdims=True)
    stats_ref[0] = peak
    stats_ref[1] = jnp.broadcast_to(total, (ROWS, LANES))


def posts_kernel(_, held_ref, allowed_ref, mine_ref, theirs_ref, *out_refs):
    peak = jnp.maximum(mine_ref[0], theirs_ref[0])
    total = mine_ref[1] * jnp.exp(mine_ref[0] - peak) + theirs_ref[1] * jnp.exp(theirs_ref[0] - peak)
    for d, out_ref in enumerate(out_refs):
        at = slice(d * ROWS, (d + 1) * ROWS)
        out_ref[...] = jnp.where(allowed_ref[at, :] > 0.5, jnp.exp(held_ref[at, :] - peak) / total, 0.0)


def spread_kernel(s_ref, *refs):
    count = len(refs) - 2
    blocks, (post_ref, copies_ref) = refs[:count], refs[count:]
    x = s_ref[1]
    rounded = jnp.concatenate([b[...] for b in blocks], axis=0).astype(jnp.bfloat16)
    for e, block in enumerate(blocks):
        at = lax.rem(x + count - e, count) * ROWS
        post_ref[pl.ds(pl.multiple_of(at, ROWS), ROWS), :] = block[...]
    for g in range(copies_ref.shape[0]):
        copies_ref[g] = rounded


def final_kernel(s_ref, post_ref, slices_ref, cos_ref, sin_ref, turned_ref, *refs):
    c = s_ref[0]
    images, (sums_ref, mine_ref, theirs_ref) = refs[:-3], refs[-3:]
    own, other = images[: len(images) // 2], images[len(images) // 2 :]
    groups = post_ref.shape[0]
    rows = groups * ROWS
    posts = [
        post_ref[:, e * ROWS : (e + 1) * ROWS, :].reshape(rows, LANES).astype(jnp.float32).T for e in range(len(own))
    ]
    posts = jnp.concatenate(posts, axis=1)
    mass = jnp.sum(posts, axis=1, keepdims=True)
    posts = posts.astype(jnp.bfloat16)
    tiles = own[0].shape[1] // ROWS
    for where, blocks in ((c, own), (1 - c, other)):
        for t in range(tiles):
            piece = jnp.concatenate(
                [b[:, t * ROWS : (t + 1) * ROWS, :].reshape(rows, LANES) for b in blocks], axis=0
            )
            sums_ref[where, :, t * LANES : (t + 1) * LANES] = jnp.dot(
                posts, piece, preferred_element_type=jnp.float32
            )
    cosine, sine = cos_ref[...], sin_ref[...]
    for t in range(tiles):
        at = slice(t * LANES, (t + 1) * LANES)
        first = sums_ref[0, :, at] - mass * slices_ref[0, 0, :, at].astype(jnp.float32)
        second = sums_ref[1, :, at] - mass * slices_ref[1, 0, :, at].astype(jnp.float32)
        grads = []
        for back in (first * cosine + second * sine, second * cosine - first * sine):
            high = back.astype(jnp.bfloat16)
            low = (back - high.astype(jnp.float32)).astype(jnp.bfloat16)
            both = jnp.concatenate([high, low], axis=0)
            grads.append(jnp.dot(turned_ref[...], both, preferred_element_type=jnp.float32) / noise_var)
        mine_ref[:, at] = jnp.where(c == 0, grads[0], grads[1])
        theirs_ref[:, at] = jnp.where(c == 0, grads[1], grads[0]).astype(jnp.bfloat16)


def weave_kernel(_, sums_ref, out_ref):
    width = out_ref.shape[0] // 2
    for part in range(2):
        for t in range(sums_ref.shape[2] // LANES):
            count = min(LANES, width - t * LANES)
            block = sums_ref[part, :, t * LANES : (t + 1) * LANES].T
            out_ref[pl.ds(2 * t * LANES + part, count, stride=2), :] = block[:count]


def join_kernel(s_ref, mine_ref, theirs_ref, out_ref):
    width = out_ref.shape[2]
    real = s_ref[0] == 0
    out_ref[:, 0, :] = jnp.where(real, mine_ref[...], theirs_ref[...])[:, :width]
    out_ref[:, 1, :] = jnp.where(real, theirs_ref[...], mine_ref[...])[:, :width]


def shards(images, shifts, inv_temp, candidates, volume, tilts, azimuth):
    i, x, c = (lax.axis_index(a) for a in ("img", "x", "c"))
    groups, across_x = lax.axis_size("img"), lax.axis_size("x")
    orients, degrees = tilts.shape
    width = volume.shape[2]
    padded = -(-width // LANES) * LANES
    tiles = padded // LANES
    scalars = jnp.stack([c, x, i]).astype(jnp.int32)

    own_temp = lax.dynamic_slice_in_dim(inv_temp, x * ROWS, ROWS, 0)
    cut = cut_images(images, shifts, scalars, width, groups)
    mine = lax.all_to_all(cut.reshape(groups, tiles * ROWS, LANES), "img", 0, 0, tiled=True)
    other = across(mine, "c", 1)

    packed = jnp.concatenate(
        [tilts.T.astype(jnp.float32), azimuth[None, :], jnp.zeros((LANES - degrees - 1, orients), jnp.float32)], axis=0
    )
    gathered = [packed]
    for d in range(1, across_x):
        gathered.append(across(packed, "x", -d))
    gathered = jnp.stack(gathered)
    pad = jnp.pad(jnp.swapaxes(volume, 0, 1), ((0, 0), (0, 0), (0, padded - width)))
    slices, half, cosine, sine = call(
        slices_kernel(width),
        (
            shape((2, across_x, orients, padded), jnp.bfloat16),
            shape((across_x, LANES)),
            shape((orients, LANES)),
            shape((orients, LANES)),
        ),
        scalars,
        gathered,
        pad,
        flops=4 * across_x * orients * degrees * padded,
    )

    partial = call(
        inner_kernel,
        shape((groups, across_x * ROWS, LANES)),
        scalars,
        mine,
        other,
        slices,
        half,
        flops=4 * groups * ROWS * padded * across_x * LANES,
    )
    partial = lax.all_to_all(partial, "img", 0, 0, tiled=True)

    ids = ((x + jnp.arange(across_x)) % across_x * 2 + c)[:, None] * orients + jnp.arange(orients)[None, :]
    allowed = jnp.any(candidates[0][:, None] == ids.reshape(1, -1), axis=0)
    allowed = allowed.astype(jnp.float32)
    allowed = jnp.broadcast_to(allowed.reshape(across_x, 1, orients), (across_x, ROWS, orients)).reshape(-1, orients)
    temp = jnp.broadcast_to(jnp.tile(own_temp, across_x)[:, None], (across_x * ROWS, LANES))
    held, stats = call(
        stats_kernel, (shape((across_x * ROWS, LANES)), shape((2, ROWS, LANES))), scalars, partial, temp, allowed
    )
    blocks = call(
        posts_kernel, [shape((ROWS, LANES))] * across_x, scalars, held, allowed, stats, across(stats, "c", 1)
    )
    blocks = [blocks[0]] + [across(blocks[d], "x", d) for d in range(1, across_x)]
    posteriors, copies = call(
        spread_kernel,
        (shape((across_x * ROWS, LANES)), shape((groups, across_x * ROWS, LANES), jnp.bfloat16)),
        scalars,
        *blocks,
    )
    posts = lax.all_to_all(copies, "img", 0, 0, tiled=True)

    mine_all = [mine]
    for d in range(1, across_x):
        mine_all.append(across(mine, "x", d))
    other_all = [other] + [across(m, "c", 1) for m in mine_all[1:]]
    turned = jnp.concatenate([tilts.T, tilts.T], axis=1)
    sums, grad, theirs = call(
        final_kernel,
        (shape((2, orients, padded)), shape((degrees, padded)), shape((degrees, padded), jnp.bfloat16)),
        scalars,
        posts,
        slices[:, :1],
        cosine,
        sine,
        turned,
        *mine_all,
        *other_all,
        flops=4 * groups * across_x * ROWS * padded * orients,
    )
    woven = call(weave_kernel, shape((2 * width, orients)), scalars, sums)
    weighted_sums = woven.reshape(width, 2, orients)

    theirs = across(theirs, "c", 1)
    grad = (grad + theirs.astype(jnp.float32)).astype(jnp.bfloat16)
    grads = [grad]
    for d in range(1, across_x):
        grads.append(across(grad, "x", d))
    grad = sum(g.astype(jnp.float32) for g in grads)
    theirs = across(grad, "c", 1)
    volume_grad = call(join_kernel, shape((degrees, 2, width)), scalars, grad, theirs)
    return posteriors, weighted_sums, volume_grad


def solution(mesh):
    ori = mesh.shape["ori"]
    finer = Mesh(mesh.devices.reshape(mesh.shape["img"], ori // 2, 2), ("img", "x", "c"))
    return jax.shard_map(
        shards,
        mesh=finer,
        in_specs=(
            P("img", None, None),
            P("img"),
            P("img"),
            P("img", None),
            P(None, None, "img"),
            P(ORI, None),
            P(ORI),
        ),
        out_specs=(P("img", ORI), P("img", None, ORI), P(None, None, "img")),
        check_vma=False,
    )
```

```python
import math

import jax
import jax.numpy as jnp
from jax import lax
from jax.experimental import pallas as pl
from jax.experimental.pallas import tpu as pltpu
from jax.sharding import Mesh
from jax.sharding import PartitionSpec as P


NSHIFT = 36
LANES = 128
ROWS = 8
ORDERS = 64
CUTS = 4
noise_var = 128.0
masked_fill = -1e30
ORI = ("x", "c")


def call(kernel, out_shape, scalars, *args, flops=0):
    scalars = scalars if isinstance(scalars, tuple) else (scalars,)
    specs = [pl.BlockSpec(memory_space=pltpu.SMEM)] * len(scalars) + [pl.BlockSpec(memory_space=pltpu.VMEM)] * len(args)
    outs = jax.tree.map(lambda _: pl.BlockSpec(memory_space=pltpu.VMEM), out_shape)
    moved = sum(a.size * a.dtype.itemsize for a in (*args, *jax.tree.leaves(out_shape)))
    return pl.pallas_call(
        kernel,
        out_shape=out_shape,
        in_specs=specs,
        out_specs=outs,
        compiler_params=pltpu.CompilerParams(vmem_limit_bytes=8 * 2**20),
        cost_estimate=pl.CostEstimate(flops=flops, transcendentals=0, bytes_accessed=moved),
    )(*scalars, *args)


def shape(dims, dtype=jnp.float32):
    return jax.ShapeDtypeStruct(dims, dtype)


def across(x, axis, turn):
    return lax.ppermute(x, axis, [(s, s ^ turn) for s in range(lax.axis_size(axis))])


def orders(start):
    lane = lax.broadcasted_iota(jnp.int32, (1, LANES), 1)
    return ((start + lane) % ORDERS - ORDERS // 2).astype(jnp.float32)


def rotate_and_cut(width, parts):
    tiles = -(-width // LANES)

    def kernel(shifts_ref, images_ref, out_ref, block, sems):
        c, x = lax.axis_index("c"), lax.axis_index("x")
        whole = images_ref.shape[2] // LANES
        bounds = [whole * k // CUTS for k in range(CUTS + 1)]
        copies = []
        for k in range(CUTS):
            at = slice(bounds[k] * LANES, bounds[k + 1] * LANES)
            copies.append(
                pltpu.make_async_copy(
                    images_ref.at[pl.ds(x * ROWS, ROWS), :, at], block.at[:, :, at], sems.at[k]
                )
            )
            copies[-1].start()
        row = lax.broadcasted_iota(jnp.int32, (ROWS, LANES), 0)
        phase = jnp.zeros((ROWS, LANES), jnp.float32)
        for n in range(ROWS):
            phase = jnp.where(row == n, shifts_ref[x * ROWS + n].astype(jnp.float32), phase)
        angles = phase * (2.0 * math.pi / NSHIFT) * orders(0)
        cosine, sine = jnp.cos(angles), jnp.sin(angles)
        a = jnp.where(c == 0, cosine, sine)
        b = jnp.where(c == 0, -sine, cosine)
        lane = lax.broadcasted_iota(jnp.int32, (ROWS, LANES), 1)
        turned, part = [], 0
        for k in range(CUTS):
            copies[k].wait()
            for tile in range(bounds[k], bounds[k + 1]):
                both = block[:, :, tile * LANES : (tile + 1) * LANES].astype(jnp.float32)
                turned.append(both[:, 0, :] * a + both[:, 1, :] * b)
            while part < parts and (part + 1) * width <= len(turned) * LANES:
                shift = (part * width) % LANES
                for t in range(tiles):
                    first = part * width // LANES + t
                    one = turned[first]
                    if shift:
                        two = turned[min(first + 1, len(turned) - 1)]
                        one = jnp.where(lane < shift, two, one)
                        one = pltpu.roll(one, LANES - shift, 1)
                    left = width - t * LANES
                    if left < LANES:
                        one = jnp.where(lane < left, one, 0.0)
                    out_ref[part, t] = one.astype(jnp.bfloat16)
                part += 1

    return kernel


def cut_images(images, shifts, width, parts):
    tiles = -(-width // LANES)
    return pl.pallas_call(
        rotate_and_cut(width, parts),
        out_shape=shape((parts, tiles, ROWS, LANES), jnp.bfloat16),
        in_specs=[pl.BlockSpec(memory_space=pltpu.SMEM), pl.BlockSpec(memory_space=pl.ANY)],
        out_specs=pl.BlockSpec(memory_space=pltpu.VMEM),
        scratch_shapes=[pltpu.VMEM((ROWS, 2, images.shape[2]), jnp.bfloat16), pltpu.SemaphoreType.DMA((CUTS,))],
        compiler_params=pltpu.CompilerParams(vmem_limit_bytes=60 * 2**20),
    )(shifts, images)


def slices_kernel(width):
    def kernel(s_ref, temp_ref, listed_ref, packed_ref, volume_ref, slices_ref, half_ref, temps_ref, allowed_ref):
        c, x = s_ref[0], s_ref[1]
        degrees = volume_ref.shape[1]
        row = lax.broadcasted_iota(jnp.int32, (ROWS, LANES), 0)
        temps = jnp.zeros((ROWS, LANES), jnp.float32)
        for n in range(ROWS):
            temps = jnp.where(row == n, temp_ref[x * ROWS + n], temps)
        listed = [
            jnp.broadcast_to(listed_ref[k : k + 1, :].astype(jnp.float32), (LANES, LANES)).T
            for k in range(listed_ref.shape[0])
        ]
        lane = lax.broadcasted_iota(jnp.int32, (1, LANES), 1)
        order = orders(s_ref[2] * width)
        for d in range(packed_ref.shape[0]):
            ids = (((x ^ d) * 2 + c) * LANES + lane).astype(jnp.float32)
            found = jnp.zeros((LANES, LANES), jnp.float32)
            for one in listed:
                found = jnp.where(one == ids, 1.0, found)
            allowed_ref[d * ROWS : (d + 1) * ROWS, :] = jnp.broadcast_to(
                jnp.max(found, axis=0, keepdims=True), (ROWS, LANES)
            )
            temps_ref[d * ROWS : (d + 1) * ROWS, :] = temps
            block = packed_ref[d].T
            angles = jnp.broadcast_to(block[:, degrees : degrees + 1], block.shape) * order
            cosine, sine = jnp.cos(angles), jnp.sin(angles)
            tilts = block[:, :degrees].astype(jnp.bfloat16)
            power = jnp.zeros_like(block)
            for t in range(volume_ref.shape[2] // LANES):
                at = slice(t * LANES, (t + 1) * LANES)
                re = jnp.dot(tilts, volume_ref[0, :, at], preferred_element_type=jnp.float32)
                im = jnp.dot(tilts, volume_ref[1, :, at], preferred_element_type=jnp.float32)
                first = (re * cosine - im * sine).astype(jnp.bfloat16)
                second = (re * sine + im * cosine).astype(jnp.bfloat16)
                slices_ref[0, d, :, at] = first
                slices_ref[1, d, :, at] = second
                power += jnp.square(first.astype(jnp.float32)) + jnp.square(second.astype(jnp.float32))
            half_ref[d : d + 1, :] = 0.5 * jnp.sum(power.T, axis=0, keepdims=True)

    return kernel


def turns_kernel(width):
    def kernel(s_ref, azimuth_ref, turn_ref):
        angles = jnp.broadcast_to(azimuth_ref[...], (LANES, LANES)).T * orders(s_ref[2] * width)
        turn_ref[0] = jnp.cos(angles)
        turn_ref[1] = jnp.sin(angles)

    return kernel


def wide(ref, rows):
    tiles = ref.shape[1] // ROWS
    pieces = [ref[:, t * ROWS : (t + 1) * ROWS, :].reshape(rows, LANES) for t in range(tiles)]
    return jnp.concatenate(pieces, axis=1)


def inner_kernel(s_ref, own_ref, other_ref, slices_ref, half_ref, out_ref):
    c = s_ref[0]
    groups = own_ref.shape[0]
    rows = groups * ROWS
    own, other = wide(own_ref, rows), wide(other_ref, rows)
    dims = (((1,), (1,)), ((), ()))
    for d in range(slices_ref.shape[1]):
        acc = lax.dot_general(own, slices_ref[c, d], dims, preferred_element_type=jnp.float32)
        acc += lax.dot_general(other, slices_ref[1 - c, d], dims, preferred_element_type=jnp.float32)
        acc = acc - half_ref[d : d + 1, :]
        out_ref[:, d * ROWS : (d + 1) * ROWS, :] = acc.reshape(groups, ROWS, LANES)


def stats_kernel(_, parts_ref, temp_ref, allowed_ref, held_ref, stats_ref):
    inner = parts_ref[0]
    for g in range(1, parts_ref.shape[0]):
        inner = inner + parts_ref[g]
    allowed = allowed_ref[...] > 0.5
    held = jnp.where(allowed, temp_ref[...] * inner / noise_var, masked_fill)
    held_ref[...] = held
    blocks = held.shape[0] // ROWS
    top = jnp.max(held.reshape(blocks, ROWS, LANES), axis=0)
    peak = jnp.broadcast_to(jnp.max(top, axis=1, keepdims=True), (ROWS, LANES))
    full = jnp.concatenate([peak] * blocks, axis=0)
    expo = jnp.where(allowed, jnp.exp(held - full), 0.0)
    total = jnp.sum(jnp.sum(expo.reshape(blocks, ROWS, LANES), axis=0), axis=1, keepdims=True)
    stats_ref[0] = peak
    stats_ref[1] = jnp.broadcast_to(total, (ROWS, LANES))


def posts_kernel(s_ref, held_ref, allowed_ref, mine_ref, theirs_ref, out_ref):
    peak = jnp.maximum(mine_ref[0], theirs_ref[0])
    total = mine_ref[1] * jnp.exp(mine_ref[0] - peak) + theirs_ref[1] * jnp.exp(theirs_ref[0] - peak)
    for d in range(out_ref.shape[1]):
        at = slice(d * ROWS, (d + 1) * ROWS)
        posts = jnp.where(allowed_ref[at, :] > 0.5, jnp.exp(held_ref[at, :] - peak) / total, 0.0)
        posts = posts.astype(jnp.bfloat16)
        for g in range(out_ref.shape[0]):
            out_ref[g, s_ref[1] ^ d] = posts


def final_kernel(s_ref, post_ref, slices_ref, turn_ref, turned_ref, *refs):
    c = s_ref[0]
    images, (sums_ref, mine_ref, theirs_ref) = refs[:-3], refs[-3:]
    own, other = images[: len(images) // 2], images[len(images) // 2 :]
    groups = post_ref.shape[0]
    rows = groups * ROWS
    posts = [
        post_ref[:, s_ref[1] ^ e].reshape(rows, LANES).astype(jnp.float32).T for e in range(len(own))
    ]
    posts = jnp.concatenate(posts, axis=1)
    mass = jnp.sum(posts, axis=1, keepdims=True)
    posts = posts.astype(jnp.bfloat16)
    tiles = own[0].shape[1] // ROWS
    for where, blocks in ((c, own), (1 - c, other)):
        for t in range(tiles):
            piece = jnp.concatenate(
                [b[:, t * ROWS : (t + 1) * ROWS, :].reshape(rows, LANES) for b in blocks], axis=0
            )
            sums_ref[where, :, t * LANES : (t + 1) * LANES] = jnp.dot(
                posts, piece, preferred_element_type=jnp.float32
            )
    cosine, sine = turn_ref[0], turn_ref[1]
    for t in range(tiles):
        at = slice(t * LANES, (t + 1) * LANES)
        first = sums_ref[0, :, at] - mass * slices_ref[0, 0, :, at].astype(jnp.float32)
        second = sums_ref[1, :, at] - mass * slices_ref[1, 0, :, at].astype(jnp.float32)
        grads = []
        for back in (first * cosine + second * sine, second * cosine - first * sine):
            high = back.astype(jnp.bfloat16)
            low = (back - high.astype(jnp.float32)).astype(jnp.bfloat16)
            both = jnp.concatenate([high, low], axis=0)
            grads.append(jnp.dot(turned_ref[...], both, preferred_element_type=jnp.float32) / noise_var)
        mine_ref[:, at] = jnp.where(c == 0, grads[0], grads[1])
        theirs_ref[:, at] = jnp.where(c == 0, grads[1], grads[0]).astype(jnp.bfloat16)


def weave_kernel(s_ref, sums_ref, post_ref, out_ref, own_ref):
    own_ref[...] = post_ref[s_ref[2]].astype(jnp.float32)
    width = out_ref.shape[0] // 2
    for part in range(2):
        for t in range(sums_ref.shape[2] // LANES):
            count = min(LANES, width - t * LANES)
            block = sums_ref[part, :, t * LANES : (t + 1) * LANES].T
            out_ref[pl.ds(2 * t * LANES + part, count, stride=2), :] = block[:count]


def join_kernel(s_ref, mine_ref, theirs_ref, out_ref):
    width = out_ref.shape[2]
    real = s_ref[0] == 0
    out_ref[:, 0, :] = jnp.where(real, mine_ref[...], theirs_ref[...])[:, :width]
    out_ref[:, 1, :] = jnp.where(real, theirs_ref[...], mine_ref[...])[:, :width]


def shards(images, shifts, inv_temp, candidates, volume, tilts, azimuth):
    i, x, c = (lax.axis_index(a) for a in ("img", "x", "c"))
    groups, across_x = lax.axis_size("img"), lax.axis_size("x")
    orients, degrees = tilts.shape
    width = volume.shape[2]
    padded = -(-width // LANES) * LANES
    tiles = padded // LANES
    scalars = jnp.stack([c, x, i]).astype(jnp.int32)

    cut = cut_images(images, shifts, width, groups)
    mine = lax.all_to_all(cut.reshape(groups, tiles * ROWS, LANES), "img", 0, 0, tiled=True)
    other = across(mine, "c", 1)

    packed = jnp.concatenate(
        [tilts.T.astype(jnp.float32), azimuth[None, :], jnp.zeros((LANES - degrees - 1, orients), jnp.float32)], axis=0
    )
    gathered = [packed]
    for d in range(1, across_x):
        gathered.append(across(packed, "x", d))
    gathered = jnp.stack(gathered)
    pad = jnp.pad(jnp.swapaxes(volume, 0, 1), ((0, 0), (0, 0), (0, padded - width)))
    slices, half, temps, allowed = call(
        slices_kernel(width),
        (
            shape((2, across_x, orients, padded), jnp.bfloat16),
            shape((across_x, LANES)),
            shape((across_x * ROWS, LANES)),
            shape((across_x * ROWS, LANES)),
        ),
        (scalars, inv_temp),
        candidates.reshape(-1, LANES),
        gathered,
        pad,
        flops=4 * across_x * orients * degrees * padded,
    )

    partial = call(
        inner_kernel,
        shape((groups, across_x * ROWS, LANES)),
        scalars,
        mine,
        other,
        slices,
        half,
        flops=4 * groups * ROWS * padded * across_x * LANES,
    )
    partial = lax.all_to_all(partial, "img", 0, 0, tiled=True)

    held, stats = call(
        stats_kernel, (shape((across_x * ROWS, LANES)), shape((2, ROWS, LANES))), scalars, partial, temps, allowed
    )
    copies = call(
        posts_kernel,
        shape((groups, across_x, ROWS, LANES), jnp.bfloat16),
        scalars,
        held,
        allowed,
        stats,
        across(stats, "c", 1),
    )
    copies = copies.reshape(groups * across_x, ROWS, LANES)
    posts = lax.all_to_all(copies, ("img", "x"), 0, 0, tiled=True)
    posts = posts.reshape(groups, across_x, ROWS, LANES)

    mine_all = [mine]
    for d in range(1, across_x):
        mine_all.append(across(mine, "x", d))
    other_all = [other] + [across(m, "c", 1) for m in mine_all[1:]]
    turned = jnp.concatenate([tilts.T, tilts.T], axis=1)
    turns = call(turns_kernel(width), shape((2, orients, LANES)), scalars, azimuth[None, :])
    sums, grad, theirs = call(
        final_kernel,
        (shape((2, orients, padded)), shape((degrees, padded)), shape((degrees, padded), jnp.bfloat16)),
        scalars,
        posts,
        slices[:, :1],
        turns,
        turned,
        *mine_all,
        *other_all,
        flops=4 * groups * across_x * ROWS * padded * orients,
    )
    woven, posteriors = call(
        weave_kernel,
        (shape((2 * width, orients)), shape((across_x * ROWS, LANES))),
        scalars,
        sums,
        posts.reshape(groups, across_x * ROWS, LANES),
    )
    weighted_sums = woven.reshape(width, 2, orients)

    theirs = across(theirs, "c", 1)
    grad = (grad + theirs.astype(jnp.float32)).astype(jnp.bfloat16)
    grads = [grad]
    for d in range(1, across_x):
        grads.append(across(grad, "x", d))
    grad = sum(g.astype(jnp.float32) for g in grads)
    theirs = across(grad, "c", 1)
    volume_grad = call(join_kernel, shape((degrees, 2, width)), scalars, grad, theirs)
    return posteriors, weighted_sums, volume_grad


def solution(mesh):
    ori = mesh.shape["ori"]
    finer = Mesh(mesh.devices.reshape(mesh.shape["img"], ori // 2, 2), ("img", "x", "c"))
    return jax.shard_map(
        shards,
        mesh=finer,
        in_specs=(
            P("img", None, None),
            P("img"),
            P("img"),
            P("img", None),
            P(None, None, "img"),
            P(ORI, None),
            P(ORI),
        ),
        out_specs=(P("img", ORI), P("img", None, ORI), P(None, None, "img")),
        check_vma=False,
    )
```

```python
import math

import jax
import jax.numpy as jnp
from jax import lax
from jax.experimental import pallas as pl
from jax.experimental.pallas import tpu as pltpu
from jax.sharding import Mesh
from jax.sharding import PartitionSpec as P


NSHIFT = 36
LANES = 128
ROWS = 8
ORDERS = 64
CUTS = 4
noise_var = 128.0
masked_fill = -1e30
ORI = ("x", "c")


def call(kernel, out_shape, scalars, *args, flops=0):
    scalars = scalars if isinstance(scalars, tuple) else (scalars,)
    specs = [pl.BlockSpec(memory_space=pltpu.SMEM)] * len(scalars) + [pl.BlockSpec(memory_space=pltpu.VMEM)] * len(args)
    outs = jax.tree.map(lambda _: pl.BlockSpec(memory_space=pltpu.VMEM), out_shape)
    moved = sum(a.size * a.dtype.itemsize for a in (*args, *jax.tree.leaves(out_shape)))
    return pl.pallas_call(
        kernel,
        out_shape=out_shape,
        in_specs=specs,
        out_specs=outs,
        compiler_params=pltpu.CompilerParams(vmem_limit_bytes=8 * 2**20),
        cost_estimate=pl.CostEstimate(flops=flops, transcendentals=0, bytes_accessed=moved),
    )(*scalars, *args)


def shape(dims, dtype=jnp.float32):
    return jax.ShapeDtypeStruct(dims, dtype)


def across(x, axis, turn):
    return lax.ppermute(x, axis, [(s, s ^ turn) for s in range(lax.axis_size(axis))])


def orders(start):
    lane = lax.broadcasted_iota(jnp.int32, (1, LANES), 1)
    return ((start + lane) % ORDERS - ORDERS // 2).astype(jnp.float32)


def rotate_and_cut(width, parts):
    tiles = -(-width // LANES)

    def kernel(shifts_ref, images_ref, out_ref, block, sems):
        c, x = lax.axis_index("c"), lax.axis_index("x")
        whole = images_ref.shape[2] // LANES
        bounds = [whole * k // CUTS for k in range(CUTS + 1)]
        copies = []
        for k in range(CUTS):
            at = slice(bounds[k] * LANES, bounds[k + 1] * LANES)
            copies.append(
                pltpu.make_async_copy(
                    images_ref.at[pl.ds(x * ROWS, ROWS), :, at], block.at[:, :, at], sems.at[k]
                )
            )
            copies[-1].start()
        row = lax.broadcasted_iota(jnp.int32, (ROWS, LANES), 0)
        phase = jnp.zeros((ROWS, LANES), jnp.float32)
        for n in range(ROWS):
            phase = jnp.where(row == n, shifts_ref[x * ROWS + n].astype(jnp.float32), phase)
        angles = phase * (2.0 * math.pi / NSHIFT) * orders(0)
        cosine, sine = jnp.cos(angles), jnp.sin(angles)
        a = jnp.where(c == 0, cosine, sine)
        b = jnp.where(c == 0, -sine, cosine)
        lane = lax.broadcasted_iota(jnp.int32, (ROWS, LANES), 1)
        turned, part = [], 0
        for k in range(CUTS):
            copies[k].wait()
            for tile in range(bounds[k], bounds[k + 1]):
                both = block[:, :, tile * LANES : (tile + 1) * LANES].astype(jnp.float32)
                turned.append(both[:, 0, :] * a + both[:, 1, :] * b)
            while part < parts and (part + 1) * width <= len(turned) * LANES:
                shift = (part * width) % LANES
                for t in range(tiles):
                    first = part * width // LANES + t
                    one = turned[first]
                    if shift:
                        two = turned[min(first + 1, len(turned) - 1)]
                        one = jnp.where(lane < shift, two, one)
                        one = pltpu.roll(one, LANES - shift, 1)
                    left = width - t * LANES
                    if left < LANES:
                        one = jnp.where(lane < left, one, 0.0)
                    out_ref[part, t] = one.astype(jnp.bfloat16)
                part += 1

    return kernel


def cut_images(images, shifts, width, parts):
    tiles = -(-width // LANES)
    return pl.pallas_call(
        rotate_and_cut(width, parts),
        out_shape=shape((parts, tiles, ROWS, LANES), jnp.bfloat16),
        in_specs=[pl.BlockSpec(memory_space=pltpu.SMEM), pl.BlockSpec(memory_space=pl.ANY)],
        out_specs=pl.BlockSpec(memory_space=pltpu.VMEM),
        scratch_shapes=[pltpu.VMEM((ROWS, 2, images.shape[2]), jnp.bfloat16), pltpu.SemaphoreType.DMA((CUTS,))],
        compiler_params=pltpu.CompilerParams(vmem_limit_bytes=60 * 2**20),
    )(shifts, images)


def slices_of(packed, volume_ref, order, slices_ref):
    degrees = volume_ref.shape[1]
    block = packed.astype(jnp.float32).T
    azimuth = sum(block[:, degrees + k : degrees + k + 1] for k in range(3))
    angles = jnp.broadcast_to(azimuth, (LANES, LANES)) * order
    cosine, sine = jnp.cos(angles), jnp.sin(angles)
    tilts = block[:, :degrees].astype(jnp.bfloat16)
    power = jnp.zeros((LANES, LANES), jnp.float32)
    for t in range(volume_ref.shape[2] // LANES):
        at = slice(t * LANES, (t + 1) * LANES)
        re = jnp.dot(tilts, volume_ref[0, :, at], preferred_element_type=jnp.float32)
        im = jnp.dot(tilts, volume_ref[1, :, at], preferred_element_type=jnp.float32)
        first = (re * cosine - im * sine).astype(jnp.bfloat16)
        second = (re * sine + im * cosine).astype(jnp.bfloat16)
        slices_ref[0, :, at] = first
        slices_ref[1, :, at] = second
        power += jnp.square(first.astype(jnp.float32)) + jnp.square(second.astype(jnp.float32))
    return 0.5 * jnp.sum(power.T, axis=0, keepdims=True)


def own_slices_kernel(width, across_x):
    def kernel(s_ref, temp_ref, listed_ref, packed_ref, volume_ref, slices_ref, half_ref, temps_ref, allowed_ref):
        c, x = s_ref[0], s_ref[1]
        row = lax.broadcasted_iota(jnp.int32, (ROWS, LANES), 0)
        temps = jnp.zeros((ROWS, LANES), jnp.float32)
        for n in range(ROWS):
            temps = jnp.where(row == n, temp_ref[x * ROWS + n], temps)
        listed = [
            jnp.broadcast_to(listed_ref[k : k + 1, :].astype(jnp.float32), (LANES, LANES)).T
            for k in range(listed_ref.shape[0])
        ]
        lane = lax.broadcasted_iota(jnp.int32, (1, LANES), 1)
        for d in range(across_x):
            ids = (((x ^ d) * 2 + c) * LANES + lane).astype(jnp.float32)
            found = jnp.zeros((LANES, LANES), jnp.float32)
            for one in listed:
                found = jnp.where(one == ids, 1.0, found)
            allowed_ref[d * ROWS : (d + 1) * ROWS, :] = jnp.broadcast_to(
                jnp.max(found, axis=0, keepdims=True), (ROWS, LANES)
            )
            temps_ref[d * ROWS : (d + 1) * ROWS, :] = temps
        half_ref[...] = slices_of(packed_ref[...], volume_ref, orders(s_ref[2] * width), slices_ref)

    return kernel


def slices_kernel(width):
    def kernel(s_ref, volume_ref, *refs):
        *blocks, slices_ref, half_ref = refs
        order = orders(s_ref[2] * width)
        for d, packed_ref in enumerate(blocks):
            half_ref[d : d + 1, :] = slices_of(packed_ref[...], volume_ref, order, slices_ref.at[d])

    return kernel


def turns_kernel(width):
    def kernel(s_ref, azimuth_ref, turn_ref):
        angles = jnp.broadcast_to(azimuth_ref[...], (LANES, LANES)).T * orders(s_ref[2] * width)
        turn_ref[0] = jnp.cos(angles)
        turn_ref[1] = jnp.sin(angles)

    return kernel


def wide(ref, rows):
    tiles = ref.shape[1] // ROWS
    pieces = [ref[:, t * ROWS : (t + 1) * ROWS, :].reshape(rows, LANES) for t in range(tiles)]
    return jnp.concatenate(pieces, axis=1)


def inner_kernel(s_ref, own_ref, other_ref, near_ref, near_half_ref, far_ref, far_half_ref, out_ref):
    c = s_ref[0]
    groups = own_ref.shape[0]
    rows = groups * ROWS
    own, other = wide(own_ref, rows), wide(other_ref, rows)
    dims = (((1,), (1,)), ((), ()))
    blocks = [(near_ref, near_half_ref[...])]
    blocks += [(far_ref.at[d], far_half_ref[d : d + 1, :]) for d in range(far_ref.shape[0])]
    for d, (slices, half) in enumerate(blocks):
        acc = lax.dot_general(own, slices[c], dims, preferred_element_type=jnp.float32)
        acc += lax.dot_general(other, slices[1 - c], dims, preferred_element_type=jnp.float32)
        acc = acc - half
        out_ref[:, d * ROWS : (d + 1) * ROWS, :] = acc.reshape(groups, ROWS, LANES)


def stats_kernel(_, parts_ref, temp_ref, allowed_ref, held_ref, stats_ref):
    inner = parts_ref[0]
    for g in range(1, parts_ref.shape[0]):
        inner = inner + parts_ref[g]
    allowed = allowed_ref[...] > 0.5
    held = jnp.where(allowed, temp_ref[...] * inner / noise_var, masked_fill)
    held_ref[...] = held
    blocks = held.shape[0] // ROWS
    top = jnp.max(held.reshape(blocks, ROWS, LANES), axis=0)
    peak = jnp.broadcast_to(jnp.max(top, axis=1, keepdims=True), (ROWS, LANES))
    full = jnp.concatenate([peak] * blocks, axis=0)
    expo = jnp.where(allowed, jnp.exp(held - full), 0.0)
    total = jnp.sum(jnp.sum(expo.reshape(blocks, ROWS, LANES), axis=0), axis=1, keepdims=True)
    stats_ref[0] = peak
    stats_ref[1] = jnp.broadcast_to(total, (ROWS, LANES))


def posts_kernel(s_ref, held_ref, allowed_ref, mine_ref, theirs_ref, out_ref):
    peak = jnp.maximum(mine_ref[0], theirs_ref[0])
    total = mine_ref[1] * jnp.exp(mine_ref[0] - peak) + theirs_ref[1] * jnp.exp(theirs_ref[0] - peak)
    for d in range(out_ref.shape[1]):
        at = slice(d * ROWS, (d + 1) * ROWS)
        posts = jnp.where(allowed_ref[at, :] > 0.5, jnp.exp(held_ref[at, :] - peak) / total, 0.0)
        posts = posts.astype(jnp.bfloat16)
        for g in range(out_ref.shape[0]):
            out_ref[g, s_ref[1] ^ d] = posts


def final_kernel(s_ref, post_ref, slices_ref, turn_ref, turned_ref, *refs):
    c = s_ref[0]
    images, (sums_ref, mine_ref, theirs_ref) = refs[:-3], refs[-3:]
    own, other = images[: len(images) // 2], images[len(images) // 2 :]
    groups = post_ref.shape[0]
    rows = groups * ROWS
    posts = [
        post_ref[:, s_ref[1] ^ e].reshape(rows, LANES).astype(jnp.float32).T for e in range(len(own))
    ]
    posts = jnp.concatenate(posts, axis=1)
    mass = jnp.sum(posts, axis=1, keepdims=True)
    posts = posts.astype(jnp.bfloat16)
    tiles = own[0].shape[1] // ROWS
    for where, blocks in ((c, own), (1 - c, other)):
        for t in range(tiles):
            piece = jnp.concatenate(
                [b[:, t * ROWS : (t + 1) * ROWS, :].reshape(rows, LANES) for b in blocks], axis=0
            )
            sums_ref[where, :, t * LANES : (t + 1) * LANES] = jnp.dot(
                posts, piece, preferred_element_type=jnp.float32
            )
    cosine, sine = turn_ref[0], turn_ref[1]
    for t in range(tiles):
        at = slice(t * LANES, (t + 1) * LANES)
        first = sums_ref[0, :, at] - mass * slices_ref[0, :, at].astype(jnp.float32)
        second = sums_ref[1, :, at] - mass * slices_ref[1, :, at].astype(jnp.float32)
        grads = []
        for back in (first * cosine + second * sine, second * cosine - first * sine):
            high = back.astype(jnp.bfloat16)
            low = (back - high.astype(jnp.float32)).astype(jnp.bfloat16)
            both = jnp.concatenate([high, low], axis=0)
            grads.append(jnp.dot(turned_ref[...], both, preferred_element_type=jnp.float32) / noise_var)
        mine_ref[:, at] = jnp.where(c == 0, grads[0], grads[1])
        theirs_ref[:, at] = jnp.where(c == 0, grads[1], grads[0]).astype(jnp.bfloat16)


def weave_kernel(s_ref, sums_ref, post_ref, out_ref, own_ref):
    own_ref[...] = post_ref[s_ref[2]].astype(jnp.float32)
    width = out_ref.shape[0] // 2
    for part in range(2):
        for t in range(sums_ref.shape[2] // LANES):
            count = min(LANES, width - t * LANES)
            block = sums_ref[part, :, t * LANES : (t + 1) * LANES].T
            out_ref[pl.ds(2 * t * LANES + part, count, stride=2), :] = block[:count]


def join_kernel(s_ref, mine_ref, theirs_ref, out_ref):
    width = out_ref.shape[2]
    real = s_ref[0] == 0
    out_ref[:, 0, :] = jnp.where(real, mine_ref[...], theirs_ref[...])[:, :width]
    out_ref[:, 1, :] = jnp.where(real, theirs_ref[...], mine_ref[...])[:, :width]


def shards(images, shifts, inv_temp, candidates, volume, tilts, azimuth):
    i, x, c = (lax.axis_index(a) for a in ("img", "x", "c"))
    groups, across_x = lax.axis_size("img"), lax.axis_size("x")
    orients, degrees = tilts.shape
    width = volume.shape[2]
    padded = -(-width // LANES) * LANES
    tiles = padded // LANES
    scalars = jnp.stack([c, x, i]).astype(jnp.int32)

    cut = cut_images(images, shifts, width, groups)
    mine = lax.all_to_all(cut.reshape(groups, tiles * ROWS, LANES), "img", 0, 0, tiled=True)
    other = across(mine, "c", 1)

    high = lax.reduce_precision(azimuth, 8, 7)
    middle = lax.reduce_precision(azimuth - high, 8, 7)
    terms = jnp.stack([high, middle, azimuth - high - middle]).astype(jnp.bfloat16)
    packed = jnp.concatenate([tilts.T, jnp.pad(terms, ((0, 2 * ROWS - 3), (0, 0)))], axis=0)
    gathered = []
    for d in range(1, across_x):
        gathered.append(across(packed, "x", d))
    pad = jnp.pad(jnp.swapaxes(volume, 0, 1), ((0, 0), (0, 0), (0, padded - width)))
    near, near_half, temps, allowed = call(
        own_slices_kernel(width, across_x),
        (
            shape((2, orients, padded), jnp.bfloat16),
            shape((1, LANES)),
            shape((across_x * ROWS, LANES)),
            shape((across_x * ROWS, LANES)),
        ),
        (scalars, inv_temp),
        candidates.reshape(-1, LANES),
        packed,
        pad,
        flops=4 * orients * degrees * padded,
    )
    far, far_half = call(
        slices_kernel(width),
        (shape((across_x - 1, 2, orients, padded), jnp.bfloat16), shape((across_x - 1, LANES))),
        scalars,
        pad,
        *gathered,
        flops=4 * (across_x - 1) * orients * degrees * padded,
    )

    partial = call(
        inner_kernel,
        shape((groups, across_x * ROWS, LANES)),
        scalars,
        mine,
        other,
        near,
        near_half,
        far,
        far_half,
        flops=4 * groups * ROWS * padded * across_x * LANES,
    )
    partial = lax.all_to_all(partial, "img", 0, 0, tiled=True)

    held, stats = call(
        stats_kernel, (shape((across_x * ROWS, LANES)), shape((2, ROWS, LANES))), scalars, partial, temps, allowed
    )
    copies = call(
        posts_kernel,
        shape((groups, across_x, ROWS, LANES), jnp.bfloat16),
        scalars,
        held,
        allowed,
        stats,
        across(stats, "c", 1),
    )
    copies = copies.reshape(groups * across_x, ROWS, LANES)
    posts = lax.all_to_all(copies, ("img", "x"), 0, 0, tiled=True)
    posts = posts.reshape(groups, across_x, ROWS, LANES)

    mine_all = [mine]
    for d in range(1, across_x):
        mine_all.append(across(mine, "x", d))
    other_all = [other] + [across(m, "c", 1) for m in mine_all[1:]]
    turned = jnp.concatenate([tilts.T, tilts.T], axis=1)
    turns = call(turns_kernel(width), shape((2, orients, LANES)), scalars, azimuth[None, :])
    sums, grad, theirs = call(
        final_kernel,
        (shape((2, orients, padded)), shape((degrees, padded)), shape((degrees, padded), jnp.bfloat16)),
        scalars,
        posts,
        near,
        turns,
        turned,
        *mine_all,
        *other_all,
        flops=4 * groups * across_x * ROWS * padded * orients,
    )
    woven, posteriors = call(
        weave_kernel,
        (shape((2 * width, orients)), shape((across_x * ROWS, LANES))),
        scalars,
        sums,
        posts.reshape(groups, across_x * ROWS, LANES),
    )
    weighted_sums = woven.reshape(width, 2, orients)

    theirs = across(theirs, "c", 1)
    grad = (grad + theirs.astype(jnp.float32)).astype(jnp.bfloat16)
    grads = [grad]
    for d in range(1, across_x):
        grads.append(across(grad, "x", d))
    grad = sum(g.astype(jnp.float32) for g in grads)
    theirs = across(grad, "c", 1)
    volume_grad = call(join_kernel, shape((degrees, 2, width)), scalars, grad, theirs)
    return posteriors, weighted_sums, volume_grad


def solution(mesh):
    ori = mesh.shape["ori"]
    finer = Mesh(mesh.devices.reshape(mesh.shape["img"], ori // 2, 2), ("img", "x", "c"))
    return jax.shard_map(
        shards,
        mesh=finer,
        in_specs=(
            P("img", None, None),
            P("img"),
            P("img"),
            P("img", None),
            P(None, None, "img"),
            P(ORI, None),
            P(ORI),
        ),
        out_specs=(P("img", ORI), P("img", None, ORI), P(None, None, "img")),
        check_vma=False,
    )
```

```python
import math

import jax
import jax.numpy as jnp
from jax import lax
from jax.experimental import pallas as pl
from jax.experimental.pallas import tpu as pltpu
from jax.sharding import Mesh
from jax.sharding import PartitionSpec as P


NSHIFT = 36
LANES = 128
ROWS = 8
ORDERS = 64
CUTS = 4
noise_var = 128.0
masked_fill = -1e30
ORI = ("x", "c")


def call(kernel, out_shape, scalars, *args, flops=0):
    scalars = scalars if isinstance(scalars, tuple) else (scalars,)
    specs = [pl.BlockSpec(memory_space=pltpu.SMEM)] * len(scalars) + [pl.BlockSpec(memory_space=pltpu.VMEM)] * len(args)
    outs = jax.tree.map(lambda _: pl.BlockSpec(memory_space=pltpu.VMEM), out_shape)
    moved = sum(a.size * a.dtype.itemsize for a in (*args, *jax.tree.leaves(out_shape)))
    return pl.pallas_call(
        kernel,
        out_shape=out_shape,
        in_specs=specs,
        out_specs=outs,
        compiler_params=pltpu.CompilerParams(vmem_limit_bytes=8 * 2**20),
        cost_estimate=pl.CostEstimate(flops=flops, transcendentals=0, bytes_accessed=moved),
    )(*scalars, *args)


def shape(dims, dtype=jnp.float32):
    return jax.ShapeDtypeStruct(dims, dtype)


def across(x, axis, turn):
    return lax.ppermute(x, axis, [(s, s ^ turn) for s in range(lax.axis_size(axis))])


def orders(start):
    lane = lax.broadcasted_iota(jnp.int32, (1, LANES), 1)
    return ((start + lane) % ORDERS - ORDERS // 2).astype(jnp.float32)


def rotate_and_cut(width, parts):
    tiles = -(-width // LANES)

    def kernel(shifts_ref, images_ref, out_ref, block, sems, spread):
        c, x = lax.axis_index("c"), lax.axis_index("x")
        whole = images_ref.shape[2] // LANES
        bounds = [whole * k // CUTS for k in range(CUTS + 1)]
        copies = []
        for k in range(CUTS):
            at = slice(bounds[k] * LANES, bounds[k + 1] * LANES)
            copies.append(
                pltpu.make_async_copy(
                    images_ref.at[pl.ds(x * ROWS, ROWS), :, at], block.at[:, :, at], sems.at[k]
                )
            )
            copies[-1].start()
        row = lax.broadcasted_iota(jnp.int32, (ROWS, LANES), 0)
        phase = jnp.zeros((ROWS, LANES), jnp.float32)
        for n in range(ROWS):
            phase = jnp.where(row == n, shifts_ref[x * ROWS + n].astype(jnp.float32), phase)
        angles = phase * (2.0 * math.pi / NSHIFT) * orders(0)
        cosine, sine = jnp.cos(angles), jnp.sin(angles)
        a = jnp.where(c == 0, cosine, sine)
        b = jnp.where(c == 0, -sine, cosine)
        lane = lax.broadcasted_iota(jnp.int32, (ROWS, LANES), 1)
        turned, part = [], 0
        for k in range(CUTS):
            copies[k].wait()
            for tile in range(bounds[k], bounds[k + 1]):
                at = slice(tile * LANES, (tile + 1) * LANES)
                for n in range(ROWS):
                    spread[tile, 2 * n : 2 * n + 2, :] = block[n, :, at].astype(jnp.float32)
            for tile in range(bounds[k], bounds[k + 1]):
                at = slice(tile * LANES, (tile + 1) * LANES)
                first, second = (spread[tile, pl.ds(p, ROWS, stride=2), :] for p in range(2))
                turned.append(first * a + second * b)
            while part < parts and (part + 1) * width <= len(turned) * LANES:
                shift = (part * width) % LANES
                for t in range(tiles):
                    first = part * width // LANES + t
                    one = turned[first]
                    if shift:
                        two = turned[min(first + 1, len(turned) - 1)]
                        one = jnp.where(lane < shift, two, one)
                        one = pltpu.roll(one, LANES - shift, 1)
                    left = width - t * LANES
                    if left < LANES:
                        one = jnp.where(lane < left, one, 0.0)
                    out_ref[part, t] = one.astype(jnp.bfloat16)
                part += 1

    return kernel


def cut_images(images, shifts, width, parts):
    tiles = -(-width // LANES)
    return pl.pallas_call(
        rotate_and_cut(width, parts),
        out_shape=shape((parts, tiles, ROWS, LANES), jnp.bfloat16),
        in_specs=[pl.BlockSpec(memory_space=pltpu.SMEM), pl.BlockSpec(memory_space=pl.ANY)],
        out_specs=pl.BlockSpec(memory_space=pltpu.VMEM),
        scratch_shapes=[pltpu.VMEM((ROWS, 2, images.shape[2]), jnp.bfloat16), pltpu.SemaphoreType.DMA((CUTS,)), pltpu.VMEM((images.shape[2] // LANES, 2 * ROWS, LANES), jnp.float32)],
        compiler_params=pltpu.CompilerParams(vmem_limit_bytes=60 * 2**20),
    )(shifts, images)


def slices_of(packed, volume_ref, order, slices_ref):
    degrees = volume_ref.shape[1]
    block = packed.astype(jnp.float32).T
    azimuth = sum(block[:, degrees + k : degrees + k + 1] for k in range(3))
    angles = jnp.broadcast_to(azimuth, (LANES, LANES)) * order
    cosine, sine = jnp.cos(angles), jnp.sin(angles)
    tilts = block[:, :degrees].astype(jnp.bfloat16)
    power = jnp.zeros((LANES, LANES), jnp.float32)
    for t in range(volume_ref.shape[2] // LANES):
        at = slice(t * LANES, (t + 1) * LANES)
        re = jnp.dot(tilts, volume_ref[0, :, at], preferred_element_type=jnp.float32)
        im = jnp.dot(tilts, volume_ref[1, :, at], preferred_element_type=jnp.float32)
        first = (re * cosine - im * sine).astype(jnp.bfloat16)
        second = (re * sine + im * cosine).astype(jnp.bfloat16)
        slices_ref[0, :, at] = first
        slices_ref[1, :, at] = second
        power += jnp.square(first.astype(jnp.float32)) + jnp.square(second.astype(jnp.float32))
    return 0.5 * jnp.sum(power.T, axis=0, keepdims=True)


def own_slices_kernel(width, across_x):
    def kernel(s_ref, temp_ref, listed_ref, packed_ref, volume_ref, slices_ref, half_ref, temps_ref, allowed_ref):
        c, x = s_ref[0], s_ref[1]
        row = lax.broadcasted_iota(jnp.int32, (ROWS, LANES), 0)
        temps = jnp.zeros((ROWS, LANES), jnp.float32)
        for n in range(ROWS):
            temps = jnp.where(row == n, temp_ref[x * ROWS + n], temps)
        listed = [
            jnp.broadcast_to(listed_ref[k : k + 1, :].astype(jnp.float32), (LANES, LANES)).T
            for k in range(listed_ref.shape[0])
        ]
        lane = lax.broadcasted_iota(jnp.int32, (1, LANES), 1)
        for d in range(across_x):
            ids = (((x ^ d) * 2 + c) * LANES + lane).astype(jnp.float32)
            found = jnp.zeros((LANES, LANES), jnp.float32)
            for one in listed:
                found = jnp.where(one == ids, 1.0, found)
            allowed_ref[d * ROWS : (d + 1) * ROWS, :] = jnp.broadcast_to(
                jnp.max(found, axis=0, keepdims=True), (ROWS, LANES)
            )
            temps_ref[d * ROWS : (d + 1) * ROWS, :] = temps
        half_ref[...] = slices_of(packed_ref[...], volume_ref, orders(s_ref[2] * width), slices_ref)

    return kernel


def slices_kernel(width):
    def kernel(s_ref, volume_ref, *refs):
        *blocks, slices_ref, half_ref = refs
        order = orders(s_ref[2] * width)
        for d, packed_ref in enumerate(blocks):
            half_ref[d : d + 1, :] = slices_of(packed_ref[...], volume_ref, order, slices_ref.at[d])

    return kernel


def turns_kernel(width):
    def kernel(s_ref, azimuth_ref, turn_ref):
        angles = jnp.broadcast_to(azimuth_ref[...], (LANES, LANES)).T * orders(s_ref[2] * width)
        turn_ref[0] = jnp.cos(angles)
        turn_ref[1] = jnp.sin(angles)

    return kernel


def wide(ref, rows):
    tiles = ref.shape[1] // ROWS
    pieces = [ref[:, t * ROWS : (t + 1) * ROWS, :].reshape(rows, LANES) for t in range(tiles)]
    return jnp.concatenate(pieces, axis=1)


def inner_kernel(s_ref, own_ref, other_ref, near_ref, near_half_ref, far_ref, far_half_ref, out_ref):
    c = s_ref[0]
    groups = own_ref.shape[0]
    rows = groups * ROWS
    own, other = wide(own_ref, rows), wide(other_ref, rows)
    dims = (((1,), (1,)), ((), ()))
    blocks = [(near_ref, near_half_ref[...])]
    blocks += [(far_ref.at[d], far_half_ref[d : d + 1, :]) for d in range(far_ref.shape[0])]
    for d, (slices, half) in enumerate(blocks):
        acc = lax.dot_general(own, slices[c], dims, preferred_element_type=jnp.float32)
        acc += lax.dot_general(other, slices[1 - c], dims, preferred_element_type=jnp.float32)
        acc = acc - half
        out_ref[:, d * ROWS : (d + 1) * ROWS, :] = acc.reshape(groups, ROWS, LANES)


def stats_kernel(_, parts_ref, temp_ref, allowed_ref, held_ref, stats_ref):
    inner = parts_ref[0]
    for g in range(1, parts_ref.shape[0]):
        inner = inner + parts_ref[g]
    allowed = allowed_ref[...] > 0.5
    held = jnp.where(allowed, temp_ref[...] * inner / noise_var, masked_fill)
    held_ref[...] = held
    blocks = held.shape[0] // ROWS
    top = jnp.max(held.reshape(blocks, ROWS, LANES), axis=0)
    peak = jnp.broadcast_to(jnp.max(top, axis=1, keepdims=True), (ROWS, LANES))
    full = jnp.concatenate([peak] * blocks, axis=0)
    expo = jnp.where(allowed, jnp.exp(held - full), 0.0)
    total = jnp.sum(jnp.sum(expo.reshape(blocks, ROWS, LANES), axis=0), axis=1, keepdims=True)
    stats_ref[0] = peak
    stats_ref[1] = jnp.broadcast_to(total, (ROWS, LANES))


def posts_kernel(s_ref, held_ref, allowed_ref, mine_ref, theirs_ref, out_ref):
    peak = jnp.maximum(mine_ref[0], theirs_ref[0])
    total = mine_ref[1] * jnp.exp(mine_ref[0] - peak) + theirs_ref[1] * jnp.exp(theirs_ref[0] - peak)
    for d in range(out_ref.shape[1]):
        at = slice(d * ROWS, (d + 1) * ROWS)
        posts = jnp.where(allowed_ref[at, :] > 0.5, jnp.exp(held_ref[at, :] - peak) / total, 0.0)
        posts = posts.astype(jnp.bfloat16)
        for g in range(out_ref.shape[0]):
            out_ref[g, s_ref[1] ^ d] = posts


def final_kernel(s_ref, post_ref, slices_ref, turn_ref, turned_ref, *refs):
    c = s_ref[0]
    images, (sums_ref, mine_ref, theirs_ref) = refs[:-3], refs[-3:]
    own, other = images[: len(images) // 2], images[len(images) // 2 :]
    groups = post_ref.shape[0]
    rows = groups * ROWS
    posts = [
        post_ref[:, s_ref[1] ^ e].reshape(rows, LANES).astype(jnp.float32).T for e in range(len(own))
    ]
    posts = jnp.concatenate(posts, axis=1)
    mass = jnp.sum(posts, axis=1, keepdims=True)
    posts = posts.astype(jnp.bfloat16)
    tiles = own[0].shape[1] // ROWS
    for where, blocks in ((c, own), (1 - c, other)):
        for t in range(tiles):
            piece = jnp.concatenate(
                [b[:, t * ROWS : (t + 1) * ROWS, :].reshape(rows, LANES) for b in blocks], axis=0
            )
            sums_ref[where, :, t * LANES : (t + 1) * LANES] = jnp.dot(
                posts, piece, preferred_element_type=jnp.float32
            )
    cosine, sine = turn_ref[0], turn_ref[1]
    for t in range(tiles):
        at = slice(t * LANES, (t + 1) * LANES)
        first = sums_ref[0, :, at] - mass * slices_ref[0, :, at].astype(jnp.float32)
        second = sums_ref[1, :, at] - mass * slices_ref[1, :, at].astype(jnp.float32)
        grads = []
        for back in (first * cosine + second * sine, second * cosine - first * sine):
            high = back.astype(jnp.bfloat16)
            low = (back - high.astype(jnp.float32)).astype(jnp.bfloat16)
            both = jnp.concatenate([high, low], axis=0)
            grads.append(jnp.dot(turned_ref[...], both, preferred_element_type=jnp.float32) / noise_var)
        mine_ref[:, at] = jnp.where(c == 0, grads[0], grads[1])
        theirs_ref[:, at] = jnp.where(c == 0, grads[1], grads[0]).astype(jnp.bfloat16)


def weave_kernel(s_ref, sums_ref, post_ref, out_ref, own_ref):
    own_ref[...] = post_ref[s_ref[2]].astype(jnp.float32)
    width = out_ref.shape[0] // 2
    for part in range(2):
        for t in range(sums_ref.shape[2] // LANES):
            count = min(LANES, width - t * LANES)
            block = sums_ref[part, :, t * LANES : (t + 1) * LANES].T
            out_ref[pl.ds(2 * t * LANES + part, count, stride=2), :] = block[:count]


def join_kernel(s_ref, mine_ref, theirs_ref, out_ref):
    width = out_ref.shape[2]
    real = s_ref[0] == 0
    out_ref[:, 0, :] = jnp.where(real, mine_ref[...], theirs_ref[...])[:, :width]
    out_ref[:, 1, :] = jnp.where(real, theirs_ref[...], mine_ref[...])[:, :width]


def shards(images, shifts, inv_temp, candidates, volume, tilts, azimuth):
    i, x, c = (lax.axis_index(a) for a in ("img", "x", "c"))
    groups, across_x = lax.axis_size("img"), lax.axis_size("x")
    orients, degrees = tilts.shape
    width = volume.shape[2]
    padded = -(-width // LANES) * LANES
    tiles = padded // LANES
    scalars = jnp.stack([c, x, i]).astype(jnp.int32)

    cut = cut_images(images, shifts, width, groups)
    mine = lax.all_to_all(cut.reshape(groups, tiles * ROWS, LANES), "img", 0, 0, tiled=True)
    other = across(mine, "c", 1)

    high = lax.reduce_precision(azimuth, 8, 7)
    middle = lax.reduce_precision(azimuth - high, 8, 7)
    terms = jnp.stack([high, middle, azimuth - high - middle]).astype(jnp.bfloat16)
    packed = jnp.concatenate([tilts.T, jnp.pad(terms, ((0, 2 * ROWS - 3), (0, 0)))], axis=0)
    gathered = []
    for d in range(1, across_x):
        gathered.append(across(packed, "x", d))
    pad = jnp.pad(jnp.swapaxes(volume, 0, 1), ((0, 0), (0, 0), (0, padded - width)))
    near, near_half, temps, allowed = call(
        own_slices_kernel(width, across_x),
        (
            shape((2, orients, padded), jnp.bfloat16),
            shape((1, LANES)),
            shape((across_x * ROWS, LANES)),
            shape((across_x * ROWS, LANES)),
        ),
        (scalars, inv_temp),
        candidates.reshape(-1, LANES),
        packed,
        pad,
        flops=4 * orients * degrees * padded,
    )
    far, far_half = call(
        slices_kernel(width),
        (shape((across_x - 1, 2, orients, padded), jnp.bfloat16), shape((across_x - 1, LANES))),
        scalars,
        pad,
        *gathered,
        flops=4 * (across_x - 1) * orients * degrees * padded,
    )

    partial = call(
        inner_kernel,
        shape((groups, across_x * ROWS, LANES)),
        scalars,
        mine,
        other,
        near,
        near_half,
        far,
        far_half,
        flops=4 * groups * ROWS * padded * across_x * LANES,
    )
    partial = lax.all_to_all(partial, "img", 0, 0, tiled=True)

    held, stats = call(
        stats_kernel, (shape((across_x * ROWS, LANES)), shape((2, ROWS, LANES))), scalars, partial, temps, allowed
    )
    copies = call(
        posts_kernel,
        shape((groups, across_x, ROWS, LANES), jnp.bfloat16),
        scalars,
        held,
        allowed,
        stats,
        across(stats, "c", 1),
    )
    copies = copies.reshape(groups * across_x, ROWS, LANES)
    posts = lax.all_to_all(copies, ("img", "x"), 0, 0, tiled=True)
    posts = posts.reshape(groups, across_x, ROWS, LANES)

    mine_all = [mine]
    for d in range(1, across_x):
        mine_all.append(across(mine, "x", d))
    other_all = [other] + [across(m, "c", 1) for m in mine_all[1:]]
    turned = jnp.concatenate([tilts.T, tilts.T], axis=1)
    turns = call(turns_kernel(width), shape((2, orients, LANES)), scalars, azimuth[None, :])
    sums, grad, theirs = call(
        final_kernel,
        (shape((2, orients, padded)), shape((degrees, padded)), shape((degrees, padded), jnp.bfloat16)),
        scalars,
        posts,
        near,
        turns,
        turned,
        *mine_all,
        *other_all,
        flops=4 * groups * across_x * ROWS * padded * orients,
    )
    woven, posteriors = call(
        weave_kernel,
        (shape((2 * width, orients)), shape((across_x * ROWS, LANES))),
        scalars,
        sums,
        posts.reshape(groups, across_x * ROWS, LANES),
    )
    weighted_sums = woven.reshape(width, 2, orients)

    theirs = across(theirs, "c", 1)
    grad = (grad + theirs.astype(jnp.float32)).astype(jnp.bfloat16)
    grads = [grad]
    for d in range(1, across_x):
        grads.append(across(grad, "x", d))
    grad = sum(g.astype(jnp.float32) for g in grads)
    theirs = across(grad, "c", 1)
    volume_grad = call(join_kernel, shape((degrees, 2, width)), scalars, grad, theirs)
    return posteriors, weighted_sums, volume_grad


def solution(mesh):
    ori = mesh.shape["ori"]
    finer = Mesh(mesh.devices.reshape(mesh.shape["img"], ori // 2, 2), ("img", "x", "c"))
    return jax.shard_map(
        shards,
        mesh=finer,
        in_specs=(
            P("img", None, None),
            P("img"),
            P("img"),
            P("img", None),
            P(None, None, "img"),
            P(ORI, None),
            P(ORI),
        ),
        out_specs=(P("img", ORI), P("img", None, ORI), P(None, None, "img")),
        check_vma=False,
    )
```

```python
import math

import jax
import jax.numpy as jnp
from jax import lax
from jax.experimental import pallas as pl
from jax.experimental.pallas import tpu as pltpu
from jax.sharding import Mesh
from jax.sharding import PartitionSpec as P


NSHIFT = 36
LANES = 128
ROWS = 8
ORDERS = 64
CUTS = 4
noise_var = 128.0
masked_fill = -1e30
ORI = ("x", "c")


def call(kernel, out_shape, scalars, *args, flops=0):
    scalars = scalars if isinstance(scalars, tuple) else (scalars,)
    specs = [pl.BlockSpec(memory_space=pltpu.SMEM)] * len(scalars) + [pl.BlockSpec(memory_space=pltpu.VMEM)] * len(args)
    outs = jax.tree.map(lambda _: pl.BlockSpec(memory_space=pltpu.VMEM), out_shape)
    moved = sum(a.size * a.dtype.itemsize for a in (*args, *jax.tree.leaves(out_shape)))
    return pl.pallas_call(
        kernel,
        out_shape=out_shape,
        in_specs=specs,
        out_specs=outs,
        compiler_params=pltpu.CompilerParams(vmem_limit_bytes=8 * 2**20),
        cost_estimate=pl.CostEstimate(flops=flops, transcendentals=0, bytes_accessed=moved),
    )(*scalars, *args)


def shape(dims, dtype=jnp.float32):
    return jax.ShapeDtypeStruct(dims, dtype)


def across(x, axis, turn):
    return lax.ppermute(x, axis, [(s, s ^ turn) for s in range(lax.axis_size(axis))])


def orders(start):
    lane = lax.broadcasted_iota(jnp.int32, (1, LANES), 1)
    return ((start + lane) % ORDERS - ORDERS // 2).astype(jnp.float32)


def rotate_and_cut(width, parts):
    tiles = -(-width // LANES)

    def kernel(shifts_ref, images_ref, out_ref, block, sems, spread):
        c, x = lax.axis_index("c"), lax.axis_index("x")
        whole = images_ref.shape[2] // LANES
        bounds = [whole * k // CUTS for k in range(CUTS + 1)]
        copies = []
        for k in range(CUTS):
            at = slice(bounds[k] * LANES, bounds[k + 1] * LANES)
            copies.append(
                pltpu.make_async_copy(
                    images_ref.at[pl.ds(x * ROWS, ROWS), :, at], block.at[:, :, at], sems.at[k]
                )
            )
            copies[-1].start()
        row = lax.broadcasted_iota(jnp.int32, (ROWS, LANES), 0)
        phase = jnp.zeros((ROWS, LANES), jnp.float32)
        for n in range(ROWS):
            phase = jnp.where(row == n, shifts_ref[x * ROWS + n].astype(jnp.float32), phase)
        angles = phase * (2.0 * math.pi / NSHIFT) * orders(0)
        cosine, sine = jnp.cos(angles), jnp.sin(angles)
        a = jnp.where(c == 0, cosine, sine)
        b = jnp.where(c == 0, -sine, cosine)
        lane = lax.broadcasted_iota(jnp.int32, (ROWS, LANES), 1)
        turned, part = [], 0
        for k in range(CUTS):
            copies[k].wait()
            for tile in range(bounds[k], bounds[k + 1]):
                at = slice(tile * LANES, (tile + 1) * LANES)
                for n in range(ROWS):
                    spread[tile, 2 * n : 2 * n + 2, :] = block[n, :, at].astype(jnp.float32)
            for tile in range(bounds[k], bounds[k + 1]):
                at = slice(tile * LANES, (tile + 1) * LANES)
                first, second = (spread[tile, pl.ds(p, ROWS, stride=2), :] for p in range(2))
                turned.append(first * a + second * b)
            while part < parts and (part + 1) * width <= len(turned) * LANES:
                shift = (part * width) % LANES
                for t in range(tiles):
                    first = part * width // LANES + t
                    one = turned[first]
                    if shift:
                        two = turned[min(first + 1, len(turned) - 1)]
                        one = jnp.where(lane < shift, two, one)
                        one = pltpu.roll(one, LANES - shift, 1)
                    left = width - t * LANES
                    if left < LANES:
                        one = jnp.where(lane < left, one, 0.0)
                    out_ref[part, t] = one.astype(jnp.bfloat16)
                part += 1

    return kernel


def cut_images(images, shifts, width, parts):
    tiles = -(-width // LANES)
    return pl.pallas_call(
        rotate_and_cut(width, parts),
        out_shape=shape((parts, tiles, ROWS, LANES), jnp.bfloat16),
        in_specs=[pl.BlockSpec(memory_space=pltpu.SMEM), pl.BlockSpec(memory_space=pl.ANY)],
        out_specs=pl.BlockSpec(memory_space=pltpu.VMEM),
        scratch_shapes=[pltpu.VMEM((ROWS, 2, images.shape[2]), jnp.bfloat16), pltpu.SemaphoreType.DMA((CUTS,)), pltpu.VMEM((images.shape[2] // LANES, 2 * ROWS, LANES), jnp.float32)],
        compiler_params=pltpu.CompilerParams(vmem_limit_bytes=60 * 2**20),
    )(shifts, images)


def slices_of(packed, volume_ref, order, slices_ref):
    degrees = volume_ref.shape[1]
    block = packed.astype(jnp.float32).T
    azimuth = sum(block[:, degrees + k : degrees + k + 1] for k in range(3))
    angles = jnp.broadcast_to(azimuth, (LANES, LANES)) * order
    cosine, sine = jnp.cos(angles), jnp.sin(angles)
    tilts = block[:, :degrees].astype(jnp.bfloat16)
    power = jnp.zeros((LANES, LANES), jnp.float32)
    for t in range(volume_ref.shape[2] // LANES):
        at = slice(t * LANES, (t + 1) * LANES)
        re = jnp.dot(tilts, volume_ref[0, :, at], preferred_element_type=jnp.float32)
        im = jnp.dot(tilts, volume_ref[1, :, at], preferred_element_type=jnp.float32)
        first = (re * cosine - im * sine).astype(jnp.bfloat16)
        second = (re * sine + im * cosine).astype(jnp.bfloat16)
        slices_ref[0, :, at] = first
        slices_ref[1, :, at] = second
        power += jnp.square(first.astype(jnp.float32)) + jnp.square(second.astype(jnp.float32))
    return 0.5 * jnp.sum(power.T, axis=0, keepdims=True)


def own_slices_kernel(width, across_x):
    def kernel(s_ref, temp_ref, listed_ref, packed_ref, volume_ref, slices_ref, half_ref, temps_ref, allowed_ref):
        c, x = s_ref[0], s_ref[1]
        row = lax.broadcasted_iota(jnp.int32, (ROWS, LANES), 0)
        temps = jnp.zeros((ROWS, LANES), jnp.float32)
        for n in range(ROWS):
            temps = jnp.where(row == n, temp_ref[x * ROWS + n], temps)
        listed = [
            jnp.broadcast_to(listed_ref[k : k + 1, :].astype(jnp.float32), (LANES, LANES)).T
            for k in range(listed_ref.shape[0])
        ]
        lane = lax.broadcasted_iota(jnp.int32, (1, LANES), 1)
        for d in range(across_x):
            ids = (((x ^ d) * 2 + c) * LANES + lane).astype(jnp.float32)
            found = jnp.zeros((LANES, LANES), jnp.float32)
            for one in listed:
                found = jnp.where(one == ids, 1.0, found)
            allowed_ref[d * ROWS : (d + 1) * ROWS, :] = jnp.broadcast_to(
                jnp.max(found, axis=0, keepdims=True), (ROWS, LANES)
            )
            temps_ref[d * ROWS : (d + 1) * ROWS, :] = temps
        half_ref[...] = slices_of(packed_ref[...], volume_ref, orders(s_ref[2] * width), slices_ref)

    return kernel


def slices_kernel(width):
    def kernel(s_ref, volume_ref, *refs):
        *blocks, slices_ref, half_ref = refs
        order = orders(s_ref[2] * width)
        for d, packed_ref in enumerate(blocks):
            half_ref[d : d + 1, :] = slices_of(packed_ref[...], volume_ref, order, slices_ref.at[d])

    return kernel


def turns_kernel(width):
    def kernel(s_ref, azimuth_ref, turn_ref):
        angles = jnp.broadcast_to(azimuth_ref[...], (LANES, LANES)).T * orders(s_ref[2] * width)
        turn_ref[0] = jnp.cos(angles)
        turn_ref[1] = jnp.sin(angles)

    return kernel


def wide(ref, rows):
    tiles = ref.shape[1] // ROWS
    pieces = [ref[:, t * ROWS : (t + 1) * ROWS, :].reshape(rows, LANES) for t in range(tiles)]
    return jnp.concatenate(pieces, axis=1)


SAME = (((1,), (1,)), ((), ()))


def inner_own_kernel(s_ref, own_ref, near_ref, near_half_ref, far_ref, far_half_ref, out_ref):
    c = s_ref[0]
    own = wide(own_ref, own_ref.shape[0] * ROWS)
    blocks = [(near_ref, near_half_ref[...])]
    blocks += [(far_ref.at[d], far_half_ref[d : d + 1, :]) for d in range(far_ref.shape[0])]
    for d, (slices, half) in enumerate(blocks):
        out_ref[d] = lax.dot_general(own, slices[c], SAME, preferred_element_type=jnp.float32) - half


def inner_kernel(s_ref, other_ref, near_ref, far_ref, half_way_ref, out_ref):
    c = s_ref[0]
    groups = other_ref.shape[0]
    other = wide(other_ref, groups * ROWS)
    for d in range(half_way_ref.shape[0]):
        slices = far_ref.at[d - 1] if d else near_ref
        acc = lax.dot_general(other, slices[1 - c], SAME, preferred_element_type=jnp.float32) + half_way_ref[d]
        out_ref[:, d * ROWS : (d + 1) * ROWS, :] = acc.reshape(groups, ROWS, LANES)


def stats_kernel(_, parts_ref, temp_ref, allowed_ref, held_ref, stats_ref):
    inner = parts_ref[0]
    for g in range(1, parts_ref.shape[0]):
        inner = inner + parts_ref[g]
    allowed = allowed_ref[...] > 0.5
    held = jnp.where(allowed, temp_ref[...] * inner / noise_var, masked_fill)
    held_ref[...] = held
    blocks = held.shape[0] // ROWS
    top = jnp.max(held.reshape(blocks, ROWS, LANES), axis=0)
    peak = jnp.broadcast_to(jnp.max(top, axis=1, keepdims=True), (ROWS, LANES))
    full = jnp.concatenate([peak] * blocks, axis=0)
    expo = jnp.where(allowed, jnp.exp(held - full), 0.0)
    total = jnp.sum(jnp.sum(expo.reshape(blocks, ROWS, LANES), axis=0), axis=1, keepdims=True)
    stats_ref[0] = peak
    stats_ref[1] = jnp.broadcast_to(total, (ROWS, LANES))


def posts_kernel(s_ref, held_ref, allowed_ref, mine_ref, theirs_ref, out_ref):
    peak = jnp.maximum(mine_ref[0], theirs_ref[0])
    total = mine_ref[1] * jnp.exp(mine_ref[0] - peak) + theirs_ref[1] * jnp.exp(theirs_ref[0] - peak)
    for d in range(out_ref.shape[1]):
        at = slice(d * ROWS, (d + 1) * ROWS)
        posts = jnp.where(allowed_ref[at, :] > 0.5, jnp.exp(held_ref[at, :] - peak) / total, 0.0)
        posts = posts.astype(jnp.bfloat16)
        for g in range(out_ref.shape[0]):
            out_ref[g, s_ref[1] ^ d] = posts


def final_kernel(s_ref, post_ref, slices_ref, turn_ref, turned_ref, *refs):
    c = s_ref[0]
    images, (sums_ref, mine_ref, theirs_ref) = refs[:-3], refs[-3:]
    own, other = images[: len(images) // 2], images[len(images) // 2 :]
    groups = post_ref.shape[0]
    rows = groups * ROWS
    posts = [
        post_ref[:, s_ref[1] ^ e].reshape(rows, LANES).astype(jnp.float32).T for e in range(len(own))
    ]
    posts = jnp.concatenate(posts, axis=1)
    mass = jnp.sum(posts, axis=1, keepdims=True)
    posts = posts.astype(jnp.bfloat16)
    tiles = own[0].shape[1] // ROWS
    for where, blocks in ((c, own), (1 - c, other)):
        for t in range(tiles):
            piece = jnp.concatenate(
                [b[:, t * ROWS : (t + 1) * ROWS, :].reshape(rows, LANES) for b in blocks], axis=0
            )
            sums_ref[where, :, t * LANES : (t + 1) * LANES] = jnp.dot(
                posts, piece, preferred_element_type=jnp.float32
            )
    cosine, sine = turn_ref[0], turn_ref[1]
    for t in range(tiles):
        at = slice(t * LANES, (t + 1) * LANES)
        first = sums_ref[0, :, at] - mass * slices_ref[0, :, at].astype(jnp.float32)
        second = sums_ref[1, :, at] - mass * slices_ref[1, :, at].astype(jnp.float32)
        grads = []
        for back in (first * cosine + second * sine, second * cosine - first * sine):
            high = back.astype(jnp.bfloat16)
            low = (back - high.astype(jnp.float32)).astype(jnp.bfloat16)
            both = jnp.concatenate([high, low], axis=0)
            grads.append(jnp.dot(turned_ref[...], both, preferred_element_type=jnp.float32) / noise_var)
        mine_ref[:, at] = jnp.where(c == 0, grads[0], grads[1])
        theirs_ref[:, at] = jnp.where(c == 0, grads[1], grads[0]).astype(jnp.bfloat16)


def weave_kernel(s_ref, sums_ref, post_ref, out_ref, own_ref):
    own_ref[...] = post_ref[s_ref[2]].astype(jnp.float32)
    width = out_ref.shape[0] // 2
    for part in range(2):
        for t in range(sums_ref.shape[2] // LANES):
            count = min(LANES, width - t * LANES)
            block = sums_ref[part, :, t * LANES : (t + 1) * LANES].T
            out_ref[pl.ds(2 * t * LANES + part, count, stride=2), :] = block[:count]


def join_kernel(s_ref, mine_ref, theirs_ref, out_ref):
    width = out_ref.shape[2]
    real = s_ref[0] == 0
    out_ref[:, 0, :] = jnp.where(real, mine_ref[...], theirs_ref[...])[:, :width]
    out_ref[:, 1, :] = jnp.where(real, theirs_ref[...], mine_ref[...])[:, :width]


def shards(images, shifts, inv_temp, candidates, volume, tilts, azimuth):
    i, x, c = (lax.axis_index(a) for a in ("img", "x", "c"))
    groups, across_x = lax.axis_size("img"), lax.axis_size("x")
    orients, degrees = tilts.shape
    width = volume.shape[2]
    padded = -(-width // LANES) * LANES
    tiles = padded // LANES
    scalars = jnp.stack([c, x, i]).astype(jnp.int32)

    cut = cut_images(images, shifts, width, groups)
    mine = lax.all_to_all(cut.reshape(groups, tiles * ROWS, LANES), "img", 0, 0, tiled=True)
    other = across(mine, "c", 1)

    high = lax.reduce_precision(azimuth, 8, 7)
    middle = lax.reduce_precision(azimuth - high, 8, 7)
    terms = jnp.stack([high, middle, azimuth - high - middle]).astype(jnp.bfloat16)
    packed = jnp.concatenate([tilts.T, jnp.pad(terms, ((0, 2 * ROWS - 3), (0, 0)))], axis=0)
    gathered = []
    for d in range(1, across_x):
        gathered.append(across(packed, "x", d))
    pad = jnp.pad(jnp.swapaxes(volume, 0, 1), ((0, 0), (0, 0), (0, padded - width)))
    near, near_half, temps, allowed = call(
        own_slices_kernel(width, across_x),
        (
            shape((2, orients, padded), jnp.bfloat16),
            shape((1, LANES)),
            shape((across_x * ROWS, LANES)),
            shape((across_x * ROWS, LANES)),
        ),
        (scalars, inv_temp),
        candidates.reshape(-1, LANES),
        packed,
        pad,
        flops=4 * orients * degrees * padded,
    )
    far, far_half = call(
        slices_kernel(width),
        (shape((across_x - 1, 2, orients, padded), jnp.bfloat16), shape((across_x - 1, LANES))),
        scalars,
        pad,
        *gathered,
        flops=4 * (across_x - 1) * orients * degrees * padded,
    )

    work = 2 * groups * ROWS * padded * across_x * LANES
    half_way = call(
        inner_own_kernel,
        shape((across_x, groups * ROWS, LANES)),
        scalars,
        mine,
        near,
        near_half,
        far,
        far_half,
        flops=work,
    )
    partial = call(
        inner_kernel,
        shape((groups, across_x * ROWS, LANES)),
        scalars,
        other,
        near,
        far,
        half_way,
        flops=work,
    )
    partial = lax.all_to_all(partial, "img", 0, 0, tiled=True)

    held, stats = call(
        stats_kernel, (shape((across_x * ROWS, LANES)), shape((2, ROWS, LANES))), scalars, partial, temps, allowed
    )
    copies = call(
        posts_kernel,
        shape((groups, across_x, ROWS, LANES), jnp.bfloat16),
        scalars,
        held,
        allowed,
        stats,
        across(stats, "c", 1),
    )
    copies = copies.reshape(groups * across_x, ROWS, LANES)
    posts = lax.all_to_all(copies, ("img", "x"), 0, 0, tiled=True)
    posts = posts.reshape(groups, across_x, ROWS, LANES)

    mine_all = [mine]
    for d in range(1, across_x):
        mine_all.append(across(mine, "x", d))
    other_all = [other] + [across(m, "c", 1) for m in mine_all[1:]]
    turned = jnp.concatenate([tilts.T, tilts.T], axis=1)
    turns = call(turns_kernel(width), shape((2, orients, LANES)), scalars, azimuth[None, :])
    sums, grad, theirs = call(
        final_kernel,
        (shape((2, orients, padded)), shape((degrees, padded)), shape((degrees, padded), jnp.bfloat16)),
        scalars,
        posts,
        near,
        turns,
        turned,
        *mine_all,
        *other_all,
        flops=4 * groups * across_x * ROWS * padded * orients,
    )
    woven, posteriors = call(
        weave_kernel,
        (shape((2 * width, orients)), shape((across_x * ROWS, LANES))),
        scalars,
        sums,
        posts.reshape(groups, across_x * ROWS, LANES),
    )
    weighted_sums = woven.reshape(width, 2, orients)

    theirs = across(theirs, "c", 1)
    grad = (grad + theirs.astype(jnp.float32)).astype(jnp.bfloat16)
    grads = [grad]
    for d in range(1, across_x):
        grads.append(across(grad, "x", d))
    grad = sum(g.astype(jnp.float32) for g in grads)
    theirs = across(grad, "c", 1)
    volume_grad = call(join_kernel, shape((degrees, 2, width)), scalars, grad, theirs)
    return posteriors, weighted_sums, volume_grad


def solution(mesh):
    ori = mesh.shape["ori"]
    finer = Mesh(mesh.devices.reshape(mesh.shape["img"], ori // 2, 2), ("img", "x", "c"))
    return jax.shard_map(
        shards,
        mesh=finer,
        in_specs=(
            P("img", None, None),
            P("img"),
            P("img"),
            P("img", None),
            P(None, None, "img"),
            P(ORI, None),
            P(ORI),
        ),
        out_specs=(P("img", ORI), P("img", None, ORI), P(None, None, "img")),
        check_vma=False,
    )
```
